32 devices in a mesh: beams: 2 (over y), freq: 4 (over z), tm: 2 (over x), sub: 2 (over core).
Axes of the slice: x: 2, y: 2, z: 4, core: 2. Of those that a mesh axis runs over, the one named last changes fastest.
Arguments:
- filterbank: bfloat16 [1024, 4096], P(('beams', 'freq', 'sub'), 'tm'), parts along dimension 0, may hold values from -8 to 8
- delay_shifts: int32 [9, 512], replicated, may hold values from 0 to 256, as said below
- pulse_filters: bfloat16 [6, 256], replicated, may hold values from -0.375 to 0.375
Outputs:
- dedispersed: float32 [1024, 4096], P(('beams', 'freq', 'sub'), 'tm'), parts along dimension 0
The draws below stay inside these ranges and needn't reach their ends.
There are 2 independent parts, one for each index of `beams`. The reference program is written for one: setup_inputs(seed, part) draws one part's arguments, and reference() takes and returns one part's arrays. A program takes and returns all parts, laid end to end along the dimension named above; an argument that names none is the same for every part. Nothing has to cross between parts.
Inputs may be any that keep to these rules, and one draw needn't show every extreme that they name: `delay_shifts`: at level l every shift lies in 0 to 2^l; trial 0 of every subband has shift 0 and its last trial shift 2^l.
All inputs are finite; a program needn't handle non-finite values.
Results may differ from the reference program's by a relative error of at most 0.0035.
Values may be sent and summed in bfloat16 or wider, within the bound.
A program may use at most 64 MiB of HBM per device.

```python
import math
import jax
import jax.numpy as jnp
import numpy as np
from jax import lax

CH_DEV = 64
GROUPS = 8
C = 512
LEVELS = 9
TW = 4096
TAPS = 256
NW = 6


def draw_filterbank(key, part):
    noise = jnp.clip(jax.random.normal(key, (C, TW), jnp.float32), -6.0, 6.0)
    return noise.astype(jnp.bfloat16)


def draw_delay_shifts(key, part):
    positions = jnp.arange(C, dtype=jnp.int32)
    stacked = []
    for level_num in range(LEVELS):
        width_now = 2 ** level_num
        band_width = 2 * width_now
        trial_num = positions % band_width
        base_shift = trial_num * width_now // (band_width - 1)
        jitter = jax.random.randint(jax.random.fold_in(key, 101 + level_num), (C,), -2, 3)
        shifted = jnp.clip(base_shift + jitter, 0, width_now)
        shifted = jnp.where(trial_num == 0, 0, jnp.where(trial_num == band_width - 1, width_now, shifted))
        stacked.append(shifted)
    return jnp.stack(stacked).astype(jnp.int32)


def scatter_about(rng, shape, deviation, most, kind=jnp.bfloat16):
    return jnp.clip(deviation * jax.random.normal(rng, shape, jnp.float32), -most, most).astype(kind)


def setup_inputs(seed: int = 0, part: int = 0) -> dict:
    key_of = jax.random.split(jax.random.key(seed), 4)
    own_keys = jax.random.split(jax.random.fold_in(key_of[3], part), 4)
    filterbank = draw_filterbank(jax.random.fold_in(jax.random.fold_in(key_of[3], part), 71), part)
    delay_shifts = draw_delay_shifts(jax.random.fold_in(key_of[3], 71), part)
    pulse_filters = scatter_about(key_of[2], (NW, TAPS), TAPS ** -0.5, 0.375)
    return dict(filterbank=filterbank, delay_shifts=delay_shifts, pulse_filters=pulse_filters)


def delayed_rows(source, amounts, out_len):

    def one_row(row_data, amount):
        return lax.dynamic_slice_in_dim(row_data, amount.astype(jnp.int32), out_len)
    return jax.vmap(one_row)(source, amounts)

def toeplitz_rows(filter_taps):
    tap_count = filter_taps.shape[0]
    extended = jnp.concatenate([filter_taps, jnp.zeros((tap_count + 1,), filter_taps.dtype)])
    tiled = jnp.tile(extended, tap_count)[:2 * tap_count * tap_count]
    return tiled.reshape(tap_count, 2 * tap_count)

def reference(filterbank, delay_shifts, pulse_filters):
    total_rows, window = filterbank.shape
    level_count = delay_shifts.shape[0]
    state = filterbank.astype(jnp.float32)
    for level_num in range(level_count):
        width_now = 2 ** level_num
        grouped = state.reshape(total_rows // (2 * width_now), 2, width_now, window)
        lower_rows = grouped[:, 0].reshape(-1, window)
        upper_rows = grouped[:, 1].reshape(-1, window)
        padded = jnp.concatenate([upper_rows, jnp.zeros((upper_rows.shape[0], width_now), jnp.float32)], axis=1)
        amounts = delay_shifts[level_num].reshape(-1, 2)
        even_rows = lower_rows + delayed_rows(padded, amounts[:, 0], window)
        odd_rows = lower_rows + delayed_rows(padded, amounts[:, 1], window)
        state = jnp.stack([even_rows, odd_rows], axis=1).reshape(total_rows, window)
    normalized = (state * (1.0 / math.sqrt(total_rows))).astype(jnp.bfloat16)
    extended = jnp.concatenate([normalized, jnp.zeros((total_rows, TAPS), jnp.bfloat16)], axis=1)
    block_count = window // TAPS
    windows = extended.reshape(total_rows, block_count + 1, TAPS)
    leading = windows[:, :block_count].reshape(-1, TAPS).astype(jnp.float32)
    trailing = windows[:, 1:].reshape(-1, TAPS).astype(jnp.float32)
    running_max = jnp.full(leading.shape, -1e+30, jnp.float32)
    running_sum = jnp.zeros(leading.shape, jnp.float32)
    for width_num in range(pulse_filters.shape[0]):
        kernel = toeplitz_rows(pulse_filters[width_num]).astype(jnp.float32)
        response = jnp.dot(leading, kernel[:, :TAPS].T, preferred_element_type=jnp.float32)
        response = response + jnp.dot(trailing, kernel[:, TAPS:].T, preferred_element_type=jnp.float32)
        energy = 0.5 * response * response
        new_max = jnp.maximum(running_max, energy)
        running_sum = running_sum * jnp.exp(running_max - new_max) + jnp.exp(energy - new_max)
        running_max = new_max
    natural_map = (jnp.log(running_sum) + running_max).reshape(total_rows, window)
    bit_count = GROUPS.bit_length() - 1
    flips = np.array([sum(((block_num >> bit_num & 1) << bit_count - 1 - bit_num for bit_num in range(bit_count))) for block_num in range(GROUPS)], dtype=np.int32)
    return natural_map.reshape(GROUPS, CH_DEV, window)[flips].reshape(total_rows, window)
```

```python
import functools
import math

import jax
import jax.numpy as jnp
from jax import lax
from jax.experimental import pallas as pl
from jax.experimental.pallas import tpu as pltpu
from jax.sharding import PartitionSpec as P

LANES = 128
PAIRS = 32
WIRE = jnp.bfloat16
EARLY = 2


def round_up(value, step):
    return -(-value // step) * step


def margin_takes(time_len, margin_len, tm_count):
    takes = []
    collected = 0
    for unused in range(min(tm_count - 1, -(-margin_len // time_len))):
        take = min(time_len, round_up(margin_len - collected, LANES))
        takes.append(take)
        collected += take
    return takes


def bit_reverse(value, bit_count):
    result = jnp.int32(0)
    for unused in range(bit_count):
        result = result * 2 + value % 2
        value = value // 2
    return result


def merge_level(shifts, src, dst, level, rows, pitch, local_width, flat_of, run):
    lanes = lax.broadcasted_iota(jnp.int32, (pitch, LANES), 1)
    log_width = local_width.bit_length() - 1
    far = 2**level >= LANES
    pairs = rows // 2
    unroll = min(PAIRS, pairs)
    run = min(run, 2 * unroll)

    def body(step, carry):
        first = step * unroll
        base = first + (first >> log_width) * local_width
        for offset in range(unroll):
            pair = first + offset
            lower = base + offset + (offset >> log_width) * local_width
            upper = lower + local_width
            kept = src[pl.ds(pl.multiple_of(lower * pitch, 8), pitch), :]
            for side in range(2):
                if (2 * offset + side) % run == 0:
                    flat = flat_of(2 * pair)
                    table = shifts.at[level, pl.ds(pl.multiple_of(flat, run), run)]
                out_row = 2 * pair + side
                amount = table[(2 * offset + side) % run]
                start = pl.multiple_of(upper * pitch, 8)
                if far:
                    start = start + (amount >> 7)
                    amount = amount & (LANES - 1)
                here = src[pl.ds(start, pitch), :]
                after = src[pl.ds(start + 1, pitch), :]
                turn = (LANES - amount) & (LANES - 1)
                moved = pltpu.roll(jnp.where(lanes >= amount, here, after), turn, 1)
                dst[pl.ds(pl.multiple_of(out_row * pitch, 8), pitch), :] = kept + moved
        return carry

    lax.fori_loop(0, pairs // unroll, body, 0)


def kernel(
    plan, shifts_in, filters_in, bank_in, out, shifts, filters, bank, main_a, main_b, tail_a, tail_b, state_a, state_b, margin,
    main_sent, main_got, tail_sent, tail_got, blocks, taps_mat,
    margin_send, margin_recv, main_send, main_recv, tail_send, tail_recv, loaded,
):
    rows, time_len, group_count, sub_count, tm_count, takes, pitch, main_pitch, tail_pitch, main_keep = plan
    level_count, all_channels = shifts.shape
    filter_count, tap_count = filters.shape
    bit_count = group_count.bit_length() - 1
    local_count = level_count - bit_count
    part_rows = rows // group_count
    freq, sub, tm = lax.axis_index("freq"), lax.axis_index("sub"), lax.axis_index("tm")
    position = freq * sub_count + sub
    own_block = bit_reverse(position, bit_count)
    hops = len(takes)

    barrier = pltpu.get_barrier_semaphore()

    def greet(step, carry):
        peer = (position + step) % group_count
        pl.semaphore_signal(
            barrier,
            inc=1,
            device_id={"freq": peer // sub_count, "sub": peer % sub_count},
            device_id_type=pl.DeviceIdType.MESH,
        )
        return carry

    for hop in range(1, hops + 1):
        for way in (-hop, hop):

            @pl.when((tm + way >= 0) & (tm + way < tm_count))
            def _():
                pl.semaphore_signal(
                    barrier, inc=1, device_id={"tm": tm + way}, device_id_type=pl.DeviceIdType.MESH
                )

    lax.fori_loop(1, group_count, greet, 0)

    loads = [
        pltpu.make_async_copy(source, target, loaded.at[index])
        for index, (source, target) in enumerate(
            ((bank_in, bank), (shifts_in, shifts), (filters_in, filters))
        )
    ]
    for load in loads:
        load.start()
    for load in loads:
        load.wait()

    own_cols = time_len // LANES
    for col in range(own_cols):
        main_a[pl.ds(col, rows, stride=main_pitch), :] = bank[:, pl.ds(col * LANES, LANES)].astype(
            jnp.float32
        )
    for col in range(main_keep, own_cols):
        tail_a[pl.ds(col - main_keep, rows, stride=tail_pitch), :] = bank[
            :, pl.ds(col * LANES, LANES)
        ].astype(jnp.float32)

    def local_level(level, ends, ends_pitch):
        src, dst = ends[level % 2], ends[1 - level % 2]
        merge_level(
            shifts, src, dst, level, rows, ends_pitch, 2**level, lambda row: position * rows + row,
            math.gcd(rows, LANES),
        )

    early = min(EARLY, local_count)
    for level in range(early):
        local_level(level, (main_a, main_b), main_pitch)

    neighbours = jnp.minimum(tm, hops) + jnp.minimum(tm_count - 1 - tm, hops)
    pl.semaphore_wait(barrier, group_count - 1 + neighbours)

    def margin_copy(hop):
        offset = sum(takes[: hop - 1])
        return pltpu.make_async_remote_copy(
            src_ref=bank.at[:, pl.ds(0, takes[hop - 1])],
            dst_ref=margin.at[:, pl.ds(offset, takes[hop - 1])],
            send_sem=margin_send.at[hop - 1],
            recv_sem=margin_recv.at[hop - 1],
            device_id={"tm": tm - hop},
            device_id_type=pl.DeviceIdType.MESH,
        )

    for hop in range(1, hops + 1):

        @pl.when(tm - hop >= 0)
        def _():
            margin_copy(hop).start()

    for level in range(early, local_count):
        local_level(level, (main_a, main_b), main_pitch)

    def packed(source, length, target):
        def pack(step, carry):
            block = bit_reverse((position + step) % group_count, bit_count)
            start = pl.multiple_of(block * length, 8)
            target[step, pl.ds(0, length), :] = source[pl.ds(start, length), :].astype(WIRE)
            return carry

        lax.fori_loop(1, group_count, pack, 0)

    def part_copy(step, slot, source, target, send_sems, recv_sems):
        peer = (position + step) % group_count
        return pltpu.make_async_remote_copy(
            src_ref=source.at[step],
            dst_ref=target.at[slot],
            send_sem=send_sems.at[step],
            recv_sem=recv_sems.at[slot],
            device_id={"freq": peer // sub_count, "sub": peer % sub_count},
            device_id_type=pl.DeviceIdType.MESH,
        )

    main_copy = functools.partial(
        part_copy, source=main_sent, target=main_got, send_sems=main_send, recv_sems=main_recv
    )
    tail_copy = functools.partial(
        part_copy, source=tail_sent, target=tail_got, send_sems=tail_send, recv_sems=tail_recv
    )

    def send_all(make):
        def send(step, carry):
            make(step, position).start()
            return carry

        lax.fori_loop(1, group_count, send, 0)

    main_len, tail_len = part_rows * main_pitch, part_rows * tail_pitch
    main_end, tail_end = (main_a, main_b)[local_count % 2], (tail_a, tail_b)[local_count % 2]
    packed(main_end, main_len, main_sent)
    send_all(main_copy)

    for hop in range(1, hops + 1):
        offset = sum(takes[: hop - 1])
        cols = range(offset // LANES, (offset + takes[hop - 1]) // LANES)

        @pl.when(tm + hop < tm_count)
        def _():
            margin_copy(hop).wait_recv()
            for col in cols:
                tail_a[pl.ds(own_cols - main_keep + col, rows, stride=tail_pitch), :] = margin[
                    :, pl.ds(col * LANES, LANES)
                ].astype(jnp.float32)

        @pl.when(tm + hop >= tm_count)
        def _():
            for col in cols:
                tail_a[pl.ds(own_cols - main_keep + col, rows, stride=tail_pitch), :] = jnp.zeros(
                    (rows, LANES), jnp.float32
                )

    for col in range(own_cols - main_keep + sum(takes) // LANES, tail_pitch):
        tail_a[pl.ds(col, rows, stride=tail_pitch), :] = jnp.zeros((rows, LANES), jnp.float32)

    for level in range(local_count):
        local_level(level, (tail_a, tail_b), tail_pitch)
    packed(tail_end, tail_len, tail_sent)
    send_all(tail_copy)

    span = tap_count + LANES
    all_taps = filters[...].astype(jnp.float32)
    for width in range(filter_count):
        row = jnp.concatenate([all_taps[width : width + 1], jnp.zeros((1, LANES), jnp.float32)], axis=1)
        spread = jnp.broadcast_to(row, (LANES, span))
        turned = pltpu.roll(spread, 0, 1, stride=1, stride_axis=0)
        taps_mat[pl.ds(width * LANES, LANES), :] = turned.astype(jnp.bfloat16)

    def place(group, main_part, tail_part):
        for row in range(part_rows):
            start = pl.multiple_of((group * part_rows + row) * pitch, 8)
            if main_part is not None:
                state_a[pl.ds(start, main_pitch), :] = main_part[row * main_pitch : (row + 1) * main_pitch]
            if tail_part is not None:
                state_a[pl.ds(start + main_keep, tail_pitch), :] = tail_part[
                    row * tail_pitch : (row + 1) * tail_pitch
                ]

    place(
        position,
        main_end[pl.ds(pl.multiple_of(own_block * main_len, 8), main_len), :],
        tail_end[pl.ds(pl.multiple_of(own_block * tail_len, 8), tail_len), :],
    )

    def take_main(step, carry):
        sender = (position + group_count - step) % group_count
        main_copy(step, sender).wait_recv()
        place(sender, main_got[sender, pl.ds(0, main_len), :].astype(jnp.float32), None)
        return carry

    def take_tail(step, carry):
        sender = (position + group_count - step) % group_count
        tail_copy(step, sender).wait_recv()
        place(sender, None, tail_got[sender, pl.ds(0, tail_len), :].astype(jnp.float32))
        return carry

    lax.fori_loop(1, group_count, take_main, 0)
    lax.fori_loop(1, group_count, take_tail, 0)
    src, dst = state_a, state_b

    for section in range(bit_count):
        level = local_count + section
        local_width = part_rows * 2**section
        log_band = local_width.bit_length()
        merge_level(
            shifts, src, dst, level, rows, pitch, local_width,
            lambda row: (row >> log_band) * 2 ** (level + 1)
            + own_block * (2 * local_width)
            + (row & (2 * local_width - 1)),
            2 * local_width,
        )
        src, dst = dst, src

    scale = 1.0 / math.sqrt(all_channels)
    reach = own_cols + tap_count // LANES
    for col in range(reach):
        blocks[pl.ds(col * rows, rows), :] = (src[pl.ds(col, rows, stride=pitch), :] * scale).astype(
            jnp.bfloat16
        )

    chunk_cols = 4
    chunk = chunk_cols * rows
    for first in range(0, own_cols, chunk_cols):
        pieces = [
            blocks[pl.ds((first + lag) * rows, chunk), :] for lag in range(tap_count // LANES + 1)
        ]
        response = lax.dot_general(
            jnp.concatenate(pieces, axis=1),
            taps_mat[...],
            (((1,), (1,)), ((), ())),
            preferred_element_type=jnp.float32,
        )
        energies = []
        for width in range(filter_count):
            part = response[:, width * LANES : (width + 1) * LANES]
            energies.append(0.5 * part * part)
        top = functools.reduce(jnp.maximum, energies)
        total = functools.reduce(jnp.add, [jnp.exp(energy - top) for energy in energies])
        result = jnp.log(total) + top
        for col in range(chunk_cols):
            out[:, pl.ds((first + col) * LANES, LANES)] = result[col * rows : (col + 1) * rows]

    for hop in range(1, hops + 1):

        @pl.when(tm - hop >= 0)
        def _():
            margin_copy(hop).wait_send()

    def finish(step, carry):
        main_copy(step, position).wait_send()
        tail_copy(step, position).wait_send()
        return carry

    lax.fori_loop(1, group_count, finish, 0)


def local(filterbank, delay_shifts, pulse_filters):
    rows, time_len = filterbank.shape
    sub_count, tm_count = lax.axis_size("sub"), lax.axis_size("tm")
    group_count = lax.axis_size("freq") * sub_count
    level_count = delay_shifts.shape[0]
    filter_count, tap_count = pulse_filters.shape
    margin_len = 2**level_count - 1 + tap_count
    takes = margin_takes(time_len, margin_len, tm_count)
    pitch = round_up(-(-(time_len + margin_len) // LANES), 8)
    own_cols = time_len // LANES
    local_count = level_count - (group_count.bit_length() - 1)
    main_pitch = round_up(own_cols, 8)
    main_keep = own_cols - -(-(2**local_count - 1) // LANES)
    tail_pitch = round_up(-(-(time_len + margin_len) // LANES) - main_keep, 8)
    pitch = max(pitch, round_up(main_keep + tail_pitch, 8))
    part_rows = rows // group_count
    main_part = round_up(part_rows * main_pitch, 16)
    tail_part = round_up(part_rows * tail_pitch, 16)
    spare = round_up(2**level_count // LANES + 2, 8)
    plan = (
        rows, time_len, group_count, sub_count, tm_count, takes, pitch, main_pitch, tail_pitch, main_keep,
    )
    reach = time_len // LANES + tap_count // LANES
    return pl.pallas_call(
        functools.partial(kernel, plan),
        out_shape=pltpu.VMEM((rows, time_len), jnp.float32),
        in_specs=[pl.BlockSpec(memory_space=pl.ANY)] * 3,
        out_specs=pl.BlockSpec(memory_space=pltpu.VMEM),
        scratch_shapes=[
            pltpu.SMEM(delay_shifts.shape, delay_shifts.dtype),
            pltpu.VMEM(pulse_filters.shape, pulse_filters.dtype),
            pltpu.VMEM(filterbank.shape, filterbank.dtype),
            pltpu.VMEM((rows * main_pitch + spare, LANES), jnp.float32),
            pltpu.VMEM((rows * main_pitch + spare, LANES), jnp.float32),
            pltpu.VMEM((rows * tail_pitch + spare, LANES), jnp.float32),
            pltpu.VMEM((rows * tail_pitch + spare, LANES), jnp.float32),
            pltpu.VMEM((rows * pitch + spare, LANES), jnp.float32),
            pltpu.VMEM((rows * pitch + spare, LANES), jnp.float32),
            pltpu.VMEM((rows, max(sum(takes), LANES)), jnp.bfloat16),
            pltpu.VMEM((group_count, main_part, LANES), WIRE),
            pltpu.VMEM((group_count, main_part, LANES), WIRE),
            pltpu.VMEM((group_count, tail_part, LANES), WIRE),
            pltpu.VMEM((group_count, tail_part, LANES), WIRE),
            pltpu.VMEM((reach * rows, LANES), jnp.bfloat16),
            pltpu.VMEM((filter_count * LANES, tap_count + LANES), jnp.bfloat16),
            pltpu.SemaphoreType.DMA((max(len(takes), 1),)),
            pltpu.SemaphoreType.DMA((max(len(takes), 1),)),
            pltpu.SemaphoreType.DMA((group_count,)),
            pltpu.SemaphoreType.DMA((group_count,)),
            pltpu.SemaphoreType.DMA((group_count,)),
            pltpu.SemaphoreType.DMA((group_count,)),
            pltpu.SemaphoreType.DMA((3,)),
        ],
        compiler_params=pltpu.CompilerParams(collective_id=0, has_side_effects=True),
        name="dedisperse",
    )(delay_shifts, pulse_filters, filterbank)


def solution(mesh):
    in_specs = (P(("beams", "freq", "sub"), "tm"), P(), P())
    out_specs = P(("beams", "freq", "sub"), "tm")
    return jax.shard_map(local, mesh=mesh, in_specs=in_specs, out_specs=out_specs, check_vma=False)
```

```python
import functools
import math

import jax
import jax.numpy as jnp
from jax import lax
from jax.experimental import pallas as pl
from jax.experimental.pallas import tpu as pltpu
from jax.sharding import PartitionSpec as P

LANES = 128
PAIRS = 32
WIRE = jnp.bfloat16
EARLY = 2


def round_up(value, step):
    return -(-value // step) * step


def margin_takes(time_len, margin_len, tm_count):
    takes = []
    collected = 0
    for unused in range(min(tm_count - 1, -(-margin_len // time_len))):
        take = min(time_len, round_up(margin_len - collected, LANES))
        takes.append(take)
        collected += take
    return takes


def bit_reverse(value, bit_count):
    result = jnp.int32(0)
    for unused in range(bit_count):
        result = result * 2 + value % 2
        value = value // 2
    return result


def merge_level(shifts, src, dst, level, rows, pitch, local_width, flat_of, run):
    lanes = lax.broadcasted_iota(jnp.int32, (pitch, LANES), 1)
    log_width = local_width.bit_length() - 1
    far = 2**level >= LANES
    pairs = rows // 2
    unroll = min(PAIRS, pairs)
    run = min(run, 2 * unroll)

    def body(step, carry):
        first = step * unroll
        base = first + (first >> log_width) * local_width
        for offset in range(unroll):
            pair = first + offset
            lower = base + offset + (offset >> log_width) * local_width
            upper = lower + local_width
            kept = src[pl.ds(pl.multiple_of(lower * pitch, 8), pitch), :]
            for side in range(2):
                if (2 * offset + side) % run == 0:
                    flat = flat_of(2 * pair)
                    table = shifts.at[level, pl.ds(pl.multiple_of(flat, run), run)]
                out_row = 2 * pair + side
                amount = table[(2 * offset + side) % run]
                start = pl.multiple_of(upper * pitch, 8)
                if far:
                    start = start + (amount >> 7)
                    amount = amount & (LANES - 1)
                here = src[pl.ds(start, pitch), :]
                after = src[pl.ds(start + 1, pitch), :]
                turn = (LANES - amount) & (LANES - 1)
                moved = pltpu.roll(jnp.where(lanes >= amount, here, after), turn, 1)
                dst[pl.ds(pl.multiple_of(out_row * pitch, 8), pitch), :] = kept + moved
        return carry

    lax.fori_loop(0, pairs // unroll, body, 0)


def kernel(
    plan, shifts_in, filters_in, bank_in, out, shifts, filters, bank, main_a, main_b, tail_a, tail_b, state_a, state_b, margin,
    main_sent, main_got, tail_sent, tail_got, blocks, taps_mat,
    margin_send, margin_recv, main_send, main_recv, tail_send, tail_recv, loaded,
):
    rows, time_len, group_count, sub_count, tm_count, takes, pitch, main_pitch, tail_pitch, main_keep = plan
    level_count, all_channels = shifts.shape
    filter_count, tap_count = filters.shape
    bit_count = group_count.bit_length() - 1
    local_count = level_count - bit_count
    part_rows = rows // group_count
    freq, sub, tm = lax.axis_index("freq"), lax.axis_index("sub"), lax.axis_index("tm")
    position = freq * sub_count + sub
    own_block = bit_reverse(position, bit_count)
    hops = len(takes)

    barrier = pltpu.get_barrier_semaphore()

    def greet(step, carry):
        peer = (position + step) % group_count
        pl.semaphore_signal(
            barrier,
            inc=1,
            device_id={"freq": peer // sub_count, "sub": peer % sub_count},
            device_id_type=pl.DeviceIdType.MESH,
        )
        return carry

    for hop in range(1, hops + 1):
        for way in (-hop, hop):

            @pl.when((tm + way >= 0) & (tm + way < tm_count))
            def _():
                pl.semaphore_signal(
                    barrier, inc=1, device_id={"tm": tm + way}, device_id_type=pl.DeviceIdType.MESH
                )

    lax.fori_loop(1, group_count, greet, 0)

    loads = [
        pltpu.make_async_copy(source, target, loaded.at[index])
        for index, (source, target) in enumerate(
            ((bank_in, bank), (shifts_in, shifts), (filters_in, filters))
        )
    ]
    for load in loads:
        load.start()
    for load in loads:
        load.wait()

    own_cols = time_len // LANES
    for col in range(own_cols):
        main_a[pl.ds(col, rows, stride=main_pitch), :] = bank[:, pl.ds(col * LANES, LANES)].astype(
            jnp.float32
        )
    for col in range(main_keep, own_cols):
        tail_a[pl.ds(col - main_keep, rows, stride=tail_pitch), :] = bank[
            :, pl.ds(col * LANES, LANES)
        ].astype(jnp.float32)

    def local_level(level, ends, ends_pitch):
        src, dst = ends[level % 2], ends[1 - level % 2]
        merge_level(
            shifts, src, dst, level, rows, ends_pitch, 2**level, lambda row: position * rows + row,
            math.gcd(rows, LANES),
        )

    early = min(EARLY, local_count)
    for level in range(early):
        local_level(level, (main_a, main_b), main_pitch)

    neighbours = jnp.minimum(tm, hops) + jnp.minimum(tm_count - 1 - tm, hops)
    pl.semaphore_wait(barrier, group_count - 1 + neighbours)

    def margin_copy(hop):
        offset = sum(takes[: hop - 1])
        return pltpu.make_async_remote_copy(
            src_ref=bank.at[:, pl.ds(0, takes[hop - 1])],
            dst_ref=margin.at[:, pl.ds(offset, takes[hop - 1])],
            send_sem=margin_send.at[hop - 1],
            recv_sem=margin_recv.at[hop - 1],
            device_id={"tm": tm - hop},
            device_id_type=pl.DeviceIdType.MESH,
        )

    for hop in range(1, hops + 1):

        @pl.when(tm - hop >= 0)
        def _():
            margin_copy(hop).start()

    for level in range(early, local_count):
        local_level(level, (main_a, main_b), main_pitch)

    def packed(source, length, target):
        def pack(step, carry):
            block = bit_reverse((position + step) % group_count, bit_count)
            start = pl.multiple_of(block * length, 8)
            target[step, pl.ds(0, length), :] = source[pl.ds(start, length), :].astype(WIRE)
            return carry

        lax.fori_loop(1, group_count, pack, 0)

    def part_copy(step, slot, source, target, send_sems, recv_sems):
        peer = (position + step) % group_count
        return pltpu.make_async_remote_copy(
            src_ref=source.at[step],
            dst_ref=target.at[slot],
            send_sem=send_sems.at[step],
            recv_sem=recv_sems.at[slot],
            device_id={"freq": peer // sub_count, "sub": peer % sub_count},
            device_id_type=pl.DeviceIdType.MESH,
        )

    main_copy = functools.partial(
        part_copy, source=main_sent, target=main_got, send_sems=main_send, recv_sems=main_recv
    )
    tail_copy = functools.partial(
        part_copy, source=tail_sent, target=tail_got, send_sems=tail_send, recv_sems=tail_recv
    )

    def send_all(make):
        def send(step, carry):
            make(step, position).start()
            return carry

        lax.fori_loop(1, group_count, send, 0)

    main_len, tail_len = part_rows * main_pitch, part_rows * tail_pitch
    main_end, tail_end = (main_a, main_b)[local_count % 2], (tail_a, tail_b)[local_count % 2]
    packed(main_end, main_len, main_sent)
    send_all(main_copy)

    for hop in range(1, hops + 1):
        offset = sum(takes[: hop - 1])
        cols = range(offset // LANES, (offset + takes[hop - 1]) // LANES)

        @pl.when(tm + hop < tm_count)
        def _():
            margin_copy(hop).wait_recv()
            for col in cols:
                tail_a[pl.ds(own_cols - main_keep + col, rows, stride=tail_pitch), :] = margin[
                    :, pl.ds(col * LANES, LANES)
                ].astype(jnp.float32)

        @pl.when(tm + hop >= tm_count)
        def _():
            for col in cols:
                tail_a[pl.ds(own_cols - main_keep + col, rows, stride=tail_pitch), :] = jnp.zeros(
                    (rows, LANES), jnp.float32
                )

    for col in range(own_cols - main_keep + sum(takes) // LANES, tail_pitch):
        tail_a[pl.ds(col, rows, stride=tail_pitch), :] = jnp.zeros((rows, LANES), jnp.float32)

    for level in range(local_count):
        local_level(level, (tail_a, tail_b), tail_pitch)
    packed(tail_end, tail_len, tail_sent)
    send_all(tail_copy)

    span = tap_count + LANES
    all_taps = filters[...].astype(jnp.float32)
    for width in range(filter_count):
        row = jnp.concatenate([all_taps[width : width + 1], jnp.zeros((1, LANES), jnp.float32)], axis=1)
        spread = jnp.broadcast_to(row, (LANES, span))
        turned = pltpu.roll(spread, 0, 1, stride=1, stride_axis=0)
        taps_mat[pl.ds(width * LANES, LANES), :] = turned.astype(jnp.bfloat16)

    def place(group, main_part, tail_part):
        for row in range(part_rows):
            start = pl.multiple_of((group * part_rows + row) * pitch, 8)
            if main_part is not None:
                state_a[pl.ds(start, main_pitch), :] = main_part[row * main_pitch : (row + 1) * main_pitch]
            if tail_part is not None:
                state_a[pl.ds(start + main_keep, tail_pitch), :] = tail_part[
                    row * tail_pitch : (row + 1) * tail_pitch
                ]

    place(
        position,
        main_end[pl.ds(pl.multiple_of(own_block * main_len, 8), main_len), :],
        tail_end[pl.ds(pl.multiple_of(own_block * tail_len, 8), tail_len), :],
    )

    def take_main(step, carry):
        sender = (position + group_count - step) % group_count
        main_copy(step, sender).wait_recv()
        place(sender, main_got[sender, pl.ds(0, main_len), :].astype(jnp.float32), None)
        return carry

    def take_tail(step, carry):
        sender = (position + group_count - step) % group_count
        tail_copy(step, sender).wait_recv()
        place(sender, None, tail_got[sender, pl.ds(0, tail_len), :].astype(jnp.float32))
        return carry

    lax.fori_loop(1, group_count, take_main, 0)
    lax.fori_loop(1, group_count, take_tail, 0)
    src, dst = state_a, state_b

    for section in range(bit_count):
        level = local_count + section
        local_width = part_rows * 2**section
        log_band = local_width.bit_length()
        merge_level(
            shifts, src, dst, level, rows, pitch, local_width,
            lambda row: (row >> log_band) * 2 ** (level + 1)
            + own_block * (2 * local_width)
            + (row & (2 * local_width - 1)),
            2 * local_width,
        )
        src, dst = dst, src

    scale = 1.0 / math.sqrt(all_channels)
    reach = own_cols + tap_count // LANES
    for col in range(reach):
        blocks[pl.ds(col * rows, rows), :] = (src[pl.ds(col, rows, stride=pitch), :] * scale).astype(
            jnp.bfloat16
        )

    chunk_cols = 4
    chunk = chunk_cols * rows
    for first in range(0, own_cols, chunk_cols):
        pieces = [
            blocks[pl.ds((first + lag) * rows, chunk), :] for lag in range(tap_count // LANES + 1)
        ]
        response = lax.dot_general(
            jnp.concatenate(pieces, axis=1),
            taps_mat[...],
            (((1,), (1,)), ((), ())),
            preferred_element_type=jnp.float32,
        )
        energies = []
        for width in range(filter_count):
            part = response[:, width * LANES : (width + 1) * LANES]
            energies.append(0.5 * part * part)
        top = functools.reduce(jnp.maximum, energies)
        total = functools.reduce(jnp.add, [jnp.exp(energy - top) for energy in energies])
        result = jnp.log(total) + top
        for col in range(chunk_cols):
            out[:, pl.ds((first + col) * LANES, LANES)] = result[col * rows : (col + 1) * rows]

    for hop in range(1, hops + 1):

        @pl.when(tm - hop >= 0)
        def _():
            margin_copy(hop).wait_send()

    def finish(step, carry):
        main_copy(step, position).wait_send()
        tail_copy(step, position).wait_send()
        return carry

    lax.fori_loop(1, group_count, finish, 0)


def relay_kernel(
    plan, shifts_in, filters_in, bank_in, out, shifts, filters, bank, main_a, main_b, tail_a, tail_b,
    state_a, state_b, margin, first_stage, halo_stage, first_sent, first_got, mid_sent, mid_got,
    tail_sent, tail_got, halo, taps_mat, margin_send, margin_recv, first_send, first_recv, mid_send,
    mid_recv, tail_send, tail_recv, halo_send, halo_recv, loaded,
):
    rows, time_len, group_count, sub_count, tm_count, own_cols, first_cols, mid_cols, tail_cols, pitch = plan
    level_count, all_channels = shifts.shape
    filter_count, tap_count = filters.shape
    bit_count = group_count.bit_length() - 1
    local_count = level_count - bit_count
    part_rows = rows // group_count
    freq, sub, tm = lax.axis_index("freq"), lax.axis_index("sub"), lax.axis_index("tm")
    position = freq * sub_count + sub
    own_block = bit_reverse(position, bit_count)
    has_next, has_last = tm + 1 < tm_count, tm > 0

    loads = [
        pltpu.make_async_copy(source, target, loaded.at[index])
        for index, (source, target) in enumerate(
            ((bank_in, bank), (shifts_in, shifts), (filters_in, filters))
        )
    ]
    for load in loads:
        load.start()

    barrier = pltpu.get_barrier_semaphore()

    def greet(step, carry):
        peer = (position + step) % group_count
        pl.semaphore_signal(
            barrier,
            inc=1,
            device_id={"freq": peer // sub_count, "sub": peer % sub_count},
            device_id_type=pl.DeviceIdType.MESH,
        )
        return carry

    lax.fori_loop(1, group_count, greet, 0)
    for way, present in ((-1, has_last), (1, has_next)):

        @pl.when(present)
        def _():
            pl.semaphore_signal(
                barrier, inc=1, device_id={"tm": tm + way}, device_id_type=pl.DeviceIdType.MESH
            )

    for load in loads:
        load.wait()

    for col in range(own_cols):
        main_a[pl.ds(col, rows, stride=own_cols), :] = bank[:, pl.ds(col * LANES, LANES)].astype(
            jnp.float32
        )

    def local_levels(ends, ends_pitch):
        for level in range(local_count):
            merge_level(
                shifts, ends[level % 2], ends[1 - level % 2], level, rows, ends_pitch, 2**level,
                lambda row: position * rows + row, math.gcd(rows, LANES),
            )
        return ends[local_count % 2]

    main_end = local_levels((main_a, main_b), own_cols)

    for row in range(rows):
        first_stage[pl.ds(row * first_cols, 8), :] = main_end[pl.ds(row * own_cols, 8), :]
    for block in range(group_count):
        length = part_rows * first_cols
        first_sent[block] = first_stage[pl.ds(block * length, length), :].astype(WIRE)
        mid_sent[block] = jnp.concatenate(
            [
                main_end[pl.ds((block * part_rows + row) * own_cols + first_cols, mid_cols), :]
                for row in range(part_rows)
            ],
            axis=0,
        ).astype(WIRE)

    def part_copy(step, slot, source, target, send_sems, recv_sems):
        peer = (position + step) % group_count
        return pltpu.make_async_remote_copy(
            src_ref=source.at[bit_reverse(peer, bit_count)],
            dst_ref=target.at[slot],
            send_sem=send_sems.at[step],
            recv_sem=recv_sems.at[slot],
            device_id={"freq": peer // sub_count, "sub": peer % sub_count},
            device_id_type=pl.DeviceIdType.MESH,
        )

    first_copy = functools.partial(
        part_copy, source=first_sent, target=first_got, send_sems=first_send, recv_sems=first_recv
    )
    mid_copy = functools.partial(
        part_copy, source=mid_sent, target=mid_got, send_sems=mid_send, recv_sems=mid_recv
    )
    tail_copy = functools.partial(
        part_copy, source=tail_sent, target=tail_got, send_sems=tail_send, recv_sems=tail_recv
    )

    def send_all(make):
        def send(step, carry):
            make(step, position).start()
            return carry

        lax.fori_loop(1, group_count, send, 0)

    margin_copy = pltpu.make_async_remote_copy(
        src_ref=bank.at[:, pl.ds(0, LANES)],
        dst_ref=margin,
        send_sem=margin_send.at[0],
        recv_sem=margin_recv.at[0],
        device_id={"tm": tm - 1},
        device_id_type=pl.DeviceIdType.MESH,
    )

    def halo_copy(slot, source):
        return pltpu.make_async_remote_copy(
            src_ref=source,
            dst_ref=halo.at[slot],
            send_sem=halo_send.at[slot],
            recv_sem=halo_recv.at[slot],
            device_id={"tm": tm - 1},
            device_id_type=pl.DeviceIdType.MESH,
        )

    neighbours = jnp.where(has_last, 1, 0) + jnp.where(has_next, 1, 0)
    pl.semaphore_wait(barrier, group_count - 1 + neighbours)

    @pl.when(has_last)
    def _():
        margin_copy.start()

    send_all(first_copy)

    @pl.when(has_last)
    def _():
        halo_copy(position, first_sent.at[own_block]).start()

    send_all(mid_copy)

    span = tap_count + LANES
    all_taps = filters[...].astype(jnp.float32)
    for width in range(filter_count):
        row = jnp.concatenate([all_taps[width : width + 1], jnp.zeros((1, LANES), jnp.float32)], axis=1)
        spread = jnp.broadcast_to(row, (LANES, span))
        turned = pltpu.roll(spread, 0, 1, stride=1, stride_axis=0)
        taps_mat[pl.ds(width * LANES, LANES), :] = turned.astype(jnp.bfloat16)

    for row in range(part_rows):
        start = pl.multiple_of((position * part_rows + row) * pitch, 8)
        state_a[pl.ds(start, own_cols), :] = main_end[
            pl.ds(pl.multiple_of((own_block * part_rows + row) * own_cols, 8), own_cols), :
        ]

    @pl.when(jnp.logical_not(has_next))
    def _():
        for row in range(rows):
            state_a[pl.ds(row * pitch + own_cols, pitch - own_cols), :] = jnp.zeros(
                (pitch - own_cols, LANES), jnp.float32
            )

    for col in range(tail_cols):
        tail_a[pl.ds(col, rows, stride=8), :] = bank[
            :, pl.ds((own_cols - tail_cols + col) * LANES, LANES)
        ].astype(jnp.float32)

    @pl.when(has_next)
    def _():
        margin_copy.wait_recv()
        tail_a[pl.ds(tail_cols, rows, stride=8), :] = margin[...].astype(jnp.float32)

    @pl.when(jnp.logical_not(has_next))
    def _():
        tail_a[pl.ds(tail_cols, rows, stride=8), :] = jnp.zeros((rows, LANES), jnp.float32)

    tail_end = local_levels((tail_a, tail_b), 8)
    for block in range(group_count):
        tail_sent[block] = jnp.concatenate(
            [tail_end[pl.ds(block * part_rows * 8 + col, part_rows, stride=8), :] for col in range(tail_cols)],
            axis=0,
        ).astype(WIRE)
    send_all(tail_copy)

    def place(group, part, col):
        for row in range(part_rows):
            start = (group * part_rows + row) * pitch + col
            state_a[pl.ds(start, 8), :] = part[row * 8 : (row + 1) * 8]

    def place_tail(group, parts):
        for col in range(tail_cols):
            start = group * part_rows * pitch + own_cols - tail_cols + col
            state_a[pl.ds(start, part_rows, stride=pitch), :] = parts[col]

    def spread_first(stage, group, got, col):
        length = part_rows * first_cols
        base = pl.multiple_of(group * (length + 8), 8)
        stage[pl.ds(base, length), :] = got.astype(jnp.float32)
        for row in range(part_rows):
            start = (group * part_rows + row) * pitch + col
            state_a[pl.ds(start, 8), :] = stage[pl.ds(base + row * first_cols, 8), :]

    place_tail(
        position,
        [
            tail_end[pl.ds(own_block * part_rows * 8 + col, part_rows, stride=8), :]
            for col in range(tail_cols)
        ],
    )

    def take_first(step, carry):
        sender = (position + group_count - step) % group_count
        first_copy(step, sender).wait_recv()

        @pl.when(has_last)
        def _():
            halo_copy(sender, first_got.at[sender]).start()

        spread_first(halo_stage, sender, first_got[sender], 0)
        return carry

    def take_mid(step, carry):
        sender = (position + group_count - step) % group_count
        mid_copy(step, sender).wait_recv()
        place(sender, mid_got[sender].astype(jnp.float32), first_cols)
        return carry

    def take_tail(step, carry):
        sender = (position + group_count - step) % group_count
        tail_copy(step, sender).wait_recv()
        part = tail_got[sender].astype(jnp.float32)
        place_tail(sender, [part[col * part_rows : (col + 1) * part_rows] for col in range(tail_cols)])
        return carry

    def take_halo(step, carry):
        sender = (position + group_count - step) % group_count
        halo_copy(sender, first_got.at[sender]).wait_recv()
        spread_first(halo_stage, sender, halo[sender], own_cols)
        return carry

    lax.fori_loop(1, group_count, take_first, 0)
    lax.fori_loop(1, group_count, take_mid, 0)
    lax.fori_loop(1, group_count, take_tail, 0)

    @pl.when(has_next)
    def _():
        lax.fori_loop(0, group_count, take_halo, 0)

    src, dst = state_a, state_b
    for section in range(bit_count):
        level = local_count + section
        local_width = part_rows * 2**section
        log_band = local_width.bit_length()
        merge_level(
            shifts, src, dst, level, rows, pitch, local_width,
            lambda row: (row >> log_band) * 2 ** (level + 1)
            + own_block * (2 * local_width)
            + (row & (2 * local_width - 1)),
            2 * local_width,
        )
        src, dst = dst, src

    scale = 1.0 / math.sqrt(all_channels)
    some = math.gcd(rows, 16)
    for first in range(0, rows, some):
        pieces = [
            jnp.concatenate(
                [
                    (src[pl.ds(row * pitch + lag, own_cols), :] * scale).astype(jnp.bfloat16)
                    for row in range(first, first + some)
                ],
                axis=0,
            )
            for lag in range(tap_count // LANES + 1)
        ]
        result = log_sum(pieces, taps_mat, filter_count)
        for index in range(some):
            row = first + index
            out[pl.ds(row // 8 * 8 * own_cols + row % 8, own_cols, stride=8), :] = result[
                index * own_cols : (index + 1) * own_cols
            ]

    @pl.when(has_last)
    def _():
        margin_copy.wait_send()

        def finish_halo(slot, carry):
            halo_copy(slot, first_got.at[slot]).wait_send()
            return carry

        lax.fori_loop(0, group_count, finish_halo, 0)

    def finish(step, carry):
        first_copy(step, position).wait_send()
        mid_copy(step, position).wait_send()
        tail_copy(step, position).wait_send()
        return carry

    lax.fori_loop(1, group_count, finish, 0)


def relay_plan(filterbank, delay_shifts, pulse_filters):
    rows, time_len = filterbank.shape
    sub_count, tm_count = lax.axis_size("sub"), lax.axis_size("tm")
    group_count = lax.axis_size("freq") * sub_count
    level_count = delay_shifts.shape[0]
    tap_count = pulse_filters.shape[1]
    local_count = level_count - (group_count.bit_length() - 1)
    own_cols = time_len // LANES
    tail_cols = 2
    first_cols = -(-(2**level_count - 2**local_count + tap_count - 1) // LANES)
    mid_cols = own_cols - first_cols - tail_cols
    pitch = own_cols + 8
    part_rows = rows // group_count
    fits = (
        part_rows % 8 == 0
        and own_cols % 8 == 0
        and 2**local_count <= LANES
        and first_cols <= 8
        and mid_cols == 8
        and tap_count % LANES == 0
        and part_rows * first_cols % 16 == 0
        and 2**level_count // LANES + 2 <= 8
    )
    plan = (
        rows, time_len, group_count, sub_count, tm_count, own_cols, first_cols, mid_cols, tail_cols, pitch,
    )
    return plan if fits else None


def relayed(plan, filterbank, delay_shifts, pulse_filters):
    rows, time_len, group_count, sub_count, tm_count, own_cols, first_cols, mid_cols, tail_cols, pitch = plan
    filter_count, tap_count = pulse_filters.shape
    part_rows = rows // group_count
    first_len, mid_len, tail_len = part_rows * first_cols, part_rows * mid_cols, part_rows * tail_cols
    spare = 8
    flat = pl.pallas_call(
        functools.partial(relay_kernel, plan),
        out_shape=pltpu.VMEM((rows * own_cols, LANES), jnp.float32),
        in_specs=[pl.BlockSpec(memory_space=pl.ANY)] * 3,
        out_specs=pl.BlockSpec(memory_space=pltpu.VMEM),
        scratch_shapes=[
            pltpu.SMEM(delay_shifts.shape, delay_shifts.dtype),
            pltpu.VMEM(pulse_filters.shape, pulse_filters.dtype),
            pltpu.VMEM(filterbank.shape, filterbank.dtype),
            pltpu.VMEM((rows * own_cols + spare, LANES), jnp.float32),
            pltpu.VMEM((rows * own_cols + spare, LANES), jnp.float32),
            pltpu.VMEM((rows * 8 + spare, LANES), jnp.float32),
            pltpu.VMEM((rows * 8 + spare, LANES), jnp.float32),
            pltpu.VMEM((rows * pitch + spare, LANES), jnp.float32),
            pltpu.VMEM((rows * pitch + spare, LANES), jnp.float32),
            pltpu.VMEM((rows, LANES), jnp.bfloat16),
            pltpu.VMEM((rows * first_cols + spare, LANES), jnp.float32),
            pltpu.VMEM((group_count * (first_len + 8), LANES), jnp.float32),
            pltpu.VMEM((group_count, first_len, LANES), WIRE),
            pltpu.VMEM((group_count, first_len, LANES), WIRE),
            pltpu.VMEM((group_count, mid_len, LANES), WIRE),
            pltpu.VMEM((group_count, mid_len, LANES), WIRE),
            pltpu.VMEM((group_count, tail_len, LANES), WIRE),
            pltpu.VMEM((group_count, tail_len, LANES), WIRE),
            pltpu.VMEM((group_count, first_len, LANES), WIRE),
            pltpu.VMEM((filter_count * LANES, tap_count + LANES), jnp.bfloat16),
            pltpu.SemaphoreType.DMA((1,)),
            pltpu.SemaphoreType.DMA((1,)),
        ]
        + [pltpu.SemaphoreType.DMA((group_count,)) for unused in range(8)]
        + [pltpu.SemaphoreType.DMA((3,))],
        compiler_params=pltpu.CompilerParams(collective_id=0, has_side_effects=True),
        name="dedisperse",
    )(delay_shifts, pulse_filters, filterbank)
    tiled = flat.reshape(rows // 8, own_cols, 8, LANES)
    return tiled.transpose(0, 2, 1, 3).reshape(rows, time_len)


def log_sum(pieces, taps_mat, filter_count):
    response = lax.dot_general(
        jnp.concatenate(pieces, axis=1),
        taps_mat[...],
        (((1,), (1,)), ((), ())),
        preferred_element_type=jnp.float32,
    )
    energies = []
    for width in range(filter_count):
        part = response[:, width * LANES : (width + 1) * LANES]
        energies.append(0.5 * part * part)
    top = functools.reduce(jnp.maximum, energies)
    total = functools.reduce(jnp.add, [jnp.exp(energy - top) for energy in energies])
    return jnp.log(total) + top


def local(filterbank, delay_shifts, pulse_filters):
    plan = relay_plan(filterbank, delay_shifts, pulse_filters)
    if plan is not None:
        return relayed(plan, filterbank, delay_shifts, pulse_filters)
    rows, time_len = filterbank.shape
    sub_count, tm_count = lax.axis_size("sub"), lax.axis_size("tm")
    group_count = lax.axis_size("freq") * sub_count
    level_count = delay_shifts.shape[0]
    filter_count, tap_count = pulse_filters.shape
    margin_len = 2**level_count - 1 + tap_count
    takes = margin_takes(time_len, margin_len, tm_count)
    pitch = round_up(-(-(time_len + margin_len) // LANES), 8)
    own_cols = time_len // LANES
    local_count = level_count - (group_count.bit_length() - 1)
    main_pitch = round_up(own_cols, 8)
    main_keep = own_cols - -(-(2**local_count - 1) // LANES)
    tail_pitch = round_up(-(-(time_len + margin_len) // LANES) - main_keep, 8)
    pitch = max(pitch, round_up(main_keep + tail_pitch, 8))
    part_rows = rows // group_count
    main_part = round_up(part_rows * main_pitch, 16)
    tail_part = round_up(part_rows * tail_pitch, 16)
    spare = round_up(2**level_count // LANES + 2, 8)
    plan = (
        rows, time_len, group_count, sub_count, tm_count, takes, pitch, main_pitch, tail_pitch, main_keep,
    )
    reach = time_len // LANES + tap_count // LANES
    return pl.pallas_call(
        functools.partial(kernel, plan),
        out_shape=pltpu.VMEM((rows, time_len), jnp.float32),
        in_specs=[pl.BlockSpec(memory_space=pl.ANY)] * 3,
        out_specs=pl.BlockSpec(memory_space=pltpu.VMEM),
        scratch_shapes=[
            pltpu.SMEM(delay_shifts.shape, delay_shifts.dtype),
            pltpu.VMEM(pulse_filters.shape, pulse_filters.dtype),
            pltpu.VMEM(filterbank.shape, filterbank.dtype),
            pltpu.VMEM((rows * main_pitch + spare, LANES), jnp.float32),
            pltpu.VMEM((rows * main_pitch + spare, LANES), jnp.float32),
            pltpu.VMEM((rows * tail_pitch + spare, LANES), jnp.float32),
            pltpu.VMEM((rows * tail_pitch + spare, LANES), jnp.float32),
            pltpu.VMEM((rows * pitch + spare, LANES), jnp.float32),
            pltpu.VMEM((rows * pitch + spare, LANES), jnp.float32),
            pltpu.VMEM((rows, max(sum(takes), LANES)), jnp.bfloat16),
            pltpu.VMEM((group_count, main_part, LANES), WIRE),
            pltpu.VMEM((group_count, main_part, LANES), WIRE),
            pltpu.VMEM((group_count, tail_part, LANES), WIRE),
            pltpu.VMEM((group_count, tail_part, LANES), WIRE),
            pltpu.VMEM((reach * rows, LANES), jnp.bfloat16),
            pltpu.VMEM((filter_count * LANES, tap_count + LANES), jnp.bfloat16),
            pltpu.SemaphoreType.DMA((max(len(takes), 1),)),
            pltpu.SemaphoreType.DMA((max(len(takes), 1),)),
            pltpu.SemaphoreType.DMA((group_count,)),
            pltpu.SemaphoreType.DMA((group_count,)),
            pltpu.SemaphoreType.DMA((group_count,)),
            pltpu.SemaphoreType.DMA((group_count,)),
            pltpu.SemaphoreType.DMA((3,)),
        ],
        compiler_params=pltpu.CompilerParams(collective_id=0, has_side_effects=True),
        name="dedisperse",
    )(delay_shifts, pulse_filters, filterbank)


def solution(mesh):
    in_specs = (P(("beams", "freq", "sub"), "tm"), P(), P())
    out_specs = P(("beams", "freq", "sub"), "tm")
    return jax.shard_map(local, mesh=mesh, in_specs=in_specs, out_specs=out_specs, check_vma=False)
```

```python
import functools
import math

import jax
import jax.numpy as jnp
from jax import lax
from jax.experimental import pallas as pl
from jax.experimental.pallas import tpu as pltpu
from jax.sharding import PartitionSpec as P

LANES = 128
PAIRS = 32
WIRE = jnp.bfloat16
EARLY = 2


def round_up(value, step):
    return -(-value // step) * step


def margin_takes(time_len, margin_len, tm_count):
    takes = []
    collected = 0
    for unused in range(min(tm_count - 1, -(-margin_len // time_len))):
        take = min(time_len, round_up(margin_len - collected, LANES))
        takes.append(take)
        collected += take
    return takes


def bit_reverse(value, bit_count):
    result = jnp.int32(0)
    for unused in range(bit_count):
        result = result * 2 + value % 2
        value = value // 2
    return result


def merge_level(shifts, src, dst, level, rows, pitch, local_width, flat_of, run, closed=False):
    lanes = lax.broadcasted_iota(jnp.int32, (pitch, LANES), 1)
    log_width = local_width.bit_length() - 1
    far = 2**level >= LANES
    inside = lax.broadcasted_iota(jnp.int32, (pitch, LANES), 0) < pitch - 1
    pairs = rows // 2
    unroll = min(PAIRS, pairs)
    run = min(run, 2 * unroll)

    def body(step, carry):
        first = step * unroll
        base = first + (first >> log_width) * local_width
        for offset in range(unroll):
            pair = first + offset
            lower = base + offset + (offset >> log_width) * local_width
            upper = lower + local_width
            kept = src[pl.ds(pl.multiple_of(lower * pitch, 8), pitch), :]
            for side in range(2):
                if (2 * offset + side) % run == 0:
                    flat = flat_of(2 * pair)
                    table = shifts.at[level, pl.ds(pl.multiple_of(flat, run), run)]
                out_row = 2 * pair + side
                amount = table[(2 * offset + side) % run]
                start = pl.multiple_of(upper * pitch, 8)
                if far:
                    start = start + (amount >> 7)
                    amount = amount & (LANES - 1)
                here = src[pl.ds(start, pitch), :]
                after = src[pl.ds(start + 1, pitch), :]
                if closed:
                    after = jnp.where(inside, after, 0.0)
                turn = (LANES - amount) & (LANES - 1)
                moved = pltpu.roll(jnp.where(lanes >= amount, here, after), turn, 1)
                dst[pl.ds(pl.multiple_of(out_row * pitch, 8), pitch), :] = kept + moved
        return carry

    lax.fori_loop(0, pairs // unroll, body, 0)


def kernel(
    plan, shifts_in, filters_in, bank_in, out, shifts, filters, bank, main_a, main_b, tail_a, tail_b, state_a, state_b, margin,
    main_sent, main_got, tail_sent, tail_got, blocks, taps_mat,
    margin_send, margin_recv, main_send, main_recv, tail_send, tail_recv, loaded,
):
    rows, time_len, group_count, sub_count, tm_count, takes, pitch, main_pitch, tail_pitch, main_keep = plan
    level_count, all_channels = shifts.shape
    filter_count, tap_count = filters.shape
    bit_count = group_count.bit_length() - 1
    local_count = level_count - bit_count
    part_rows = rows // group_count
    freq, sub, tm = lax.axis_index("freq"), lax.axis_index("sub"), lax.axis_index("tm")
    position = freq * sub_count + sub
    own_block = bit_reverse(position, bit_count)
    hops = len(takes)

    barrier = pltpu.get_barrier_semaphore()

    def greet(step, carry):
        peer = (position + step) % group_count
        pl.semaphore_signal(
            barrier,
            inc=1,
            device_id={"freq": peer // sub_count, "sub": peer % sub_count},
            device_id_type=pl.DeviceIdType.MESH,
        )
        return carry

    for hop in range(1, hops + 1):
        for way in (-hop, hop):

            @pl.when((tm + way >= 0) & (tm + way < tm_count))
            def _():
                pl.semaphore_signal(
                    barrier, inc=1, device_id={"tm": tm + way}, device_id_type=pl.DeviceIdType.MESH
                )

    lax.fori_loop(1, group_count, greet, 0)

    loads = [
        pltpu.make_async_copy(source, target, loaded.at[index])
        for index, (source, target) in enumerate(
            ((bank_in, bank), (shifts_in, shifts), (filters_in, filters))
        )
    ]
    for load in loads:
        load.start()
    for load in loads:
        load.wait()

    own_cols = time_len // LANES
    for col in range(own_cols):
        main_a[pl.ds(col, rows, stride=main_pitch), :] = bank[:, pl.ds(col * LANES, LANES)].astype(
            jnp.float32
        )
    for col in range(main_keep, own_cols):
        tail_a[pl.ds(col - main_keep, rows, stride=tail_pitch), :] = bank[
            :, pl.ds(col * LANES, LANES)
        ].astype(jnp.float32)

    def local_level(level, ends, ends_pitch):
        src, dst = ends[level % 2], ends[1 - level % 2]
        merge_level(
            shifts, src, dst, level, rows, ends_pitch, 2**level, lambda row: position * rows + row,
            math.gcd(rows, LANES),
        )

    early = min(EARLY, local_count)
    for level in range(early):
        local_level(level, (main_a, main_b), main_pitch)

    neighbours = jnp.minimum(tm, hops) + jnp.minimum(tm_count - 1 - tm, hops)
    pl.semaphore_wait(barrier, group_count - 1 + neighbours)

    def margin_copy(hop):
        offset = sum(takes[: hop - 1])
        return pltpu.make_async_remote_copy(
            src_ref=bank.at[:, pl.ds(0, takes[hop - 1])],
            dst_ref=margin.at[:, pl.ds(offset, takes[hop - 1])],
            send_sem=margin_send.at[hop - 1],
            recv_sem=margin_recv.at[hop - 1],
            device_id={"tm": tm - hop},
            device_id_type=pl.DeviceIdType.MESH,
        )

    for hop in range(1, hops + 1):

        @pl.when(tm - hop >= 0)
        def _():
            margin_copy(hop).start()

    for level in range(early, local_count):
        local_level(level, (main_a, main_b), main_pitch)

    def packed(source, length, target):
        def pack(step, carry):
            block = bit_reverse((position + step) % group_count, bit_count)
            start = pl.multiple_of(block * length, 8)
            target[step, pl.ds(0, length), :] = source[pl.ds(start, length), :].astype(WIRE)
            return carry

        lax.fori_loop(1, group_count, pack, 0)

    def part_copy(step, slot, source, target, send_sems, recv_sems):
        peer = (position + step) % group_count
        return pltpu.make_async_remote_copy(
            src_ref=source.at[step],
            dst_ref=target.at[slot],
            send_sem=send_sems.at[step],
            recv_sem=recv_sems.at[slot],
            device_id={"freq": peer // sub_count, "sub": peer % sub_count},
            device_id_type=pl.DeviceIdType.MESH,
        )

    main_copy = functools.partial(
        part_copy, source=main_sent, target=main_got, send_sems=main_send, recv_sems=main_recv
    )
    tail_copy = functools.partial(
        part_copy, source=tail_sent, target=tail_got, send_sems=tail_send, recv_sems=tail_recv
    )

    def send_all(make):
        def send(step, carry):
            make(step, position).start()
            return carry

        lax.fori_loop(1, group_count, send, 0)

    main_len, tail_len = part_rows * main_pitch, part_rows * tail_pitch
    main_end, tail_end = (main_a, main_b)[local_count % 2], (tail_a, tail_b)[local_count % 2]
    packed(main_end, main_len, main_sent)
    send_all(main_copy)

    for hop in range(1, hops + 1):
        offset = sum(takes[: hop - 1])
        cols = range(offset // LANES, (offset + takes[hop - 1]) // LANES)

        @pl.when(tm + hop < tm_count)
        def _():
            margin_copy(hop).wait_recv()
            for col in cols:
                tail_a[pl.ds(own_cols - main_keep + col, rows, stride=tail_pitch), :] = margin[
                    :, pl.ds(col * LANES, LANES)
                ].astype(jnp.float32)

        @pl.when(tm + hop >= tm_count)
        def _():
            for col in cols:
                tail_a[pl.ds(own_cols - main_keep + col, rows, stride=tail_pitch), :] = jnp.zeros(
                    (rows, LANES), jnp.float32
                )

    for col in range(own_cols - main_keep + sum(takes) // LANES, tail_pitch):
        tail_a[pl.ds(col, rows, stride=tail_pitch), :] = jnp.zeros((rows, LANES), jnp.float32)

    for level in range(local_count):
        local_level(level, (tail_a, tail_b), tail_pitch)
    packed(tail_end, tail_len, tail_sent)
    send_all(tail_copy)

    span = tap_count + LANES
    all_taps = filters[...].astype(jnp.float32)
    for width in range(filter_count):
        row = jnp.concatenate([all_taps[width : width + 1], jnp.zeros((1, LANES), jnp.float32)], axis=1)
        spread = jnp.broadcast_to(row, (LANES, span))
        turned = pltpu.roll(spread, 0, 1, stride=1, stride_axis=0)
        taps_mat[pl.ds(width * LANES, LANES), :] = turned.astype(jnp.bfloat16)

    def place(group, main_part, tail_part):
        for row in range(part_rows):
            start = pl.multiple_of((group * part_rows + row) * pitch, 8)
            if main_part is not None:
                state_a[pl.ds(start, main_pitch), :] = main_part[row * main_pitch : (row + 1) * main_pitch]
            if tail_part is not None:
                state_a[pl.ds(start + main_keep, tail_pitch), :] = tail_part[
                    row * tail_pitch : (row + 1) * tail_pitch
                ]

    place(
        position,
        main_end[pl.ds(pl.multiple_of(own_block * main_len, 8), main_len), :],
        tail_end[pl.ds(pl.multiple_of(own_block * tail_len, 8), tail_len), :],
    )

    def take_main(step, carry):
        sender = (position + group_count - step) % group_count
        main_copy(step, sender).wait_recv()
        place(sender, main_got[sender, pl.ds(0, main_len), :].astype(jnp.float32), None)
        return carry

    def take_tail(step, carry):
        sender = (position + group_count - step) % group_count
        tail_copy(step, sender).wait_recv()
        place(sender, None, tail_got[sender, pl.ds(0, tail_len), :].astype(jnp.float32))
        return carry

    lax.fori_loop(1, group_count, take_main, 0)
    lax.fori_loop(1, group_count, take_tail, 0)
    src, dst = state_a, state_b

    for section in range(bit_count):
        level = local_count + section
        local_width = part_rows * 2**section
        log_band = local_width.bit_length()
        merge_level(
            shifts, src, dst, level, rows, pitch, local_width,
            lambda row: (row >> log_band) * 2 ** (level + 1)
            + own_block * (2 * local_width)
            + (row & (2 * local_width - 1)),
            2 * local_width,
        )
        src, dst = dst, src

    scale = 1.0 / math.sqrt(all_channels)
    reach = own_cols + tap_count // LANES
    for col in range(reach):
        blocks[pl.ds(col * rows, rows), :] = (src[pl.ds(col, rows, stride=pitch), :] * scale).astype(
            jnp.bfloat16
        )

    chunk_cols = 4
    chunk = chunk_cols * rows
    for first in range(0, own_cols, chunk_cols):
        pieces = [
            blocks[pl.ds((first + lag) * rows, chunk), :] for lag in range(tap_count // LANES + 1)
        ]
        response = lax.dot_general(
            jnp.concatenate(pieces, axis=1),
            taps_mat[...],
            (((1,), (1,)), ((), ())),
            preferred_element_type=jnp.float32,
        )
        energies = []
        for width in range(filter_count):
            part = response[:, width * LANES : (width + 1) * LANES]
            energies.append(0.5 * part * part)
        top = functools.reduce(jnp.maximum, energies)
        total = functools.reduce(jnp.add, [jnp.exp(energy - top) for energy in energies])
        result = jnp.log(total) + top
        for col in range(chunk_cols):
            out[:, pl.ds((first + col) * LANES, LANES)] = result[col * rows : (col + 1) * rows]

    for hop in range(1, hops + 1):

        @pl.when(tm - hop >= 0)
        def _():
            margin_copy(hop).wait_send()

    def finish(step, carry):
        main_copy(step, position).wait_send()
        tail_copy(step, position).wait_send()
        return carry

    lax.fori_loop(1, group_count, finish, 0)


def nearest(position, step, bit_count):
    result, unit = jnp.int32(0), 1
    for unused in range(bit_count):
        result = result + (position // unit + step // unit) % 2 * unit
        unit *= 2
    return result


def relay_kernel(
    plan, shifts_in, filters_in, bank_in, out, shifts, filters, bank, main_a, main_b, spill_a, spill_b,
    state_a, state_b, first_stage, halo_stage, sent, got, halo, taps_mat, main_send, main_recv,
    first_send, first_recv, halo_send, halo_recv, loaded,
):
    rows, time_len, group_count, sub_count, tm_count, own_cols, first_cols, pitch = plan
    level_count, all_channels = shifts.shape
    filter_count, tap_count = filters.shape
    bit_count = group_count.bit_length() - 1
    local_count = level_count - bit_count
    part_rows = rows // group_count
    freq, sub, tm = lax.axis_index("freq"), lax.axis_index("sub"), lax.axis_index("tm")
    position = freq * sub_count + sub
    own_block = bit_reverse(position, bit_count)
    has_next, has_last = tm + 1 < tm_count, tm > 0
    first_len, main_len = part_rows * first_cols, part_rows * own_cols
    kept_cols = first_cols - 1
    edge_cols = own_cols - kept_cols - 8
    rest_len = round_up(part_rows * (8 + edge_cols), 16)
    lanes = lax.broadcasted_iota(jnp.int32, (part_rows, LANES), 1)
    spill_lane = LANES - 2**local_count

    loads = [
        pltpu.make_async_copy(source, target, loaded.at[index])
        for index, (source, target) in enumerate(
            ((bank_in, bank), (shifts_in, shifts), (filters_in, filters))
        )
    ]
    for load in loads:
        load.start()

    barrier = pltpu.get_barrier_semaphore()

    def greet(step, carry):
        peer = (position + step) % group_count
        pl.semaphore_signal(
            barrier,
            inc=1,
            device_id={"freq": peer // sub_count, "sub": peer % sub_count},
            device_id_type=pl.DeviceIdType.MESH,
        )
        return carry

    lax.fori_loop(1, group_count, greet, 0)
    for way, present in ((-1, has_last), (1, has_next)):

        @pl.when(present)
        def _():
            pl.semaphore_signal(
                barrier, inc=1, device_id={"tm": tm + way}, device_id_type=pl.DeviceIdType.MESH
            )

    for load in loads:
        load.wait()

    def local_levels(ends, ends_pitch, closed):
        for level in range(local_count):
            merge_level(
                shifts, ends[level % 2], ends[1 - level % 2], level, rows, ends_pitch, 2**level,
                lambda row: position * rows + row, math.gcd(rows, LANES), closed,
            )
        return ends[local_count % 2]

    def part_copy(step, slot, send_sems, recv_sems, start, length):
        peer = (position + step) % group_count
        return pltpu.make_async_remote_copy(
            src_ref=sent.at[bit_reverse(peer, bit_count), pl.ds(start, length)],
            dst_ref=got.at[slot, pl.ds(start, length)],
            send_sem=send_sems.at[step],
            recv_sem=recv_sems.at[slot],
            device_id={"freq": peer // sub_count, "sub": peer % sub_count},
            device_id_type=pl.DeviceIdType.MESH,
        )

    main_copy = functools.partial(
        part_copy, send_sems=main_send, recv_sems=main_recv, start=0, length=main_len
    )
    rest_copy = functools.partial(
        part_copy, send_sems=main_send, recv_sems=main_recv, start=0, length=rest_len
    )
    first_copy = functools.partial(
        part_copy, send_sems=first_send, recv_sems=first_recv, start=main_len, length=first_len
    )

    def send_all(make):
        def send(step, carry):
            make(step, position).start()
            return carry

        lax.fori_loop(1, group_count, send, 0)

    def halo_copy(slot, source):
        return pltpu.make_async_remote_copy(
            src_ref=source,
            dst_ref=halo.at[slot],
            send_sem=halo_send.at[slot],
            recv_sem=halo_recv.at[slot],
            device_id={"tm": tm - 1},
            device_id_type=pl.DeviceIdType.MESH,
        )

    def wait_all():
        neighbours = jnp.where(has_last, 1, 0) + jnp.where(has_next, 1, 0)
        pl.semaphore_wait(barrier, group_count - 1 + neighbours)

    @pl.when(has_last)
    def _():
        spill_a[pl.ds(0, rows, stride=8), :] = jnp.zeros((rows, LANES), jnp.float32)
        for col in range(7):
            spill_a[pl.ds(col + 1, rows, stride=8), :] = bank[:, pl.ds(col * LANES, LANES)].astype(
                jnp.float32
            )
        spill_end = local_levels((spill_a, spill_b), 8, False)
        for row in range(rows):
            first_stage[pl.ds(row * first_cols, 8), :] = spill_end[pl.ds(row * 8, 8), :]
        wide = lax.broadcasted_iota(jnp.int32, (rows, LANES), 1)
        first_stage[pl.ds(0, rows, stride=first_cols), :] = jnp.where(
            wide < spill_lane,
            spill_end[pl.ds(first_cols, rows, stride=8), :],
            spill_end[pl.ds(0, rows, stride=8), :],
        )
        for block in range(group_count):
            sent[block, pl.ds(main_len, first_len), :] = first_stage[
                pl.ds(block * first_len, first_len), :
            ].astype(WIRE)
        wait_all()
        send_all(first_copy)
        halo_copy(position, sent.at[own_block, pl.ds(main_len, first_len)]).start()

    for col in range(own_cols):
        main_a[pl.ds(col, rows, stride=own_cols), :] = bank[:, pl.ds(col * LANES, LANES)].astype(
            jnp.float32
        )
    main_end = local_levels((main_a, main_b), own_cols, True)

    @pl.when(jnp.logical_not(has_last))
    def _():
        for block in range(group_count):
            sent[block, pl.ds(0, main_len), :] = main_end[pl.ds(block * main_len, main_len), :].astype(WIRE)
        wait_all()
        send_all(main_copy)

    @pl.when(has_last)
    def _():
        for block in range(group_count):
            first = block * part_rows
            pieces = [
                main_end[pl.ds((first + row) * own_cols + kept_cols, 8), :] for row in range(part_rows)
            ]
            for col in range(own_cols - edge_cols, own_cols):
                pieces.append(main_end[pl.ds(first * own_cols + col, part_rows, stride=own_cols), :])
            for unused in range((rest_len - part_rows * (8 + edge_cols)) // 8):
                pieces.append(jnp.zeros((8, LANES), jnp.float32))
            sent[block, pl.ds(0, rest_len), :] = jnp.concatenate(pieces, axis=0).astype(WIRE)
        send_all(rest_copy)

    span = tap_count + LANES
    all_taps = filters[...].astype(jnp.float32)
    for width in range(filter_count):
        row = jnp.concatenate([all_taps[width : width + 1], jnp.zeros((1, LANES), jnp.float32)], axis=1)
        spread = jnp.broadcast_to(row, (LANES, span))
        turned = pltpu.roll(spread, 0, 1, stride=1, stride_axis=0)
        taps_mat[pl.ds(width * LANES, LANES), :] = turned.astype(jnp.bfloat16)

    for row in range(part_rows):
        start = pl.multiple_of((position * part_rows + row) * pitch, 8)
        state_a[pl.ds(start, own_cols), :] = main_end[
            pl.ds(pl.multiple_of((own_block * part_rows + row) * own_cols, 8), own_cols), :
        ]

    @pl.when(jnp.logical_not(has_next))
    def _():
        for row in range(rows):
            state_a[pl.ds(row * pitch + own_cols, pitch - own_cols), :] = jnp.zeros(
                (pitch - own_cols, LANES), jnp.float32
            )

    def spread(group, part, col):
        base = pl.multiple_of(group * (first_len + 8), 8)
        halo_stage[pl.ds(base, first_len), :] = part.astype(jnp.float32)
        for row in range(part_rows):
            start = (group * part_rows + row) * pitch + col
            state_a[pl.ds(start, 8), :] = halo_stage[pl.ds(base + row * first_cols + 1, 8), :]
        return halo_stage[pl.ds(base, part_rows, stride=first_cols), :]

    def forwarded(sender):
        return halo_copy(sender, got.at[sender, pl.ds(main_len, first_len)])

    def take_first(step, carry):
        sender = nearest(position, step, bit_count)
        first_copy(step, sender).wait_recv()
        forwarded(sender).start()
        spread(sender, got[sender, pl.ds(main_len, first_len), :], 0)
        return carry

    def take_rest(step, carry):
        sender = nearest(position, step, bit_count)
        rest_copy(step, sender).wait_recv()
        part = got[sender, pl.ds(0, rest_len), :].astype(jnp.float32)
        for row in range(part_rows):
            start = (sender * part_rows + row) * pitch + kept_cols
            state_a[pl.ds(start, 8), :] = part[row * 8 : (row + 1) * 8]
        for edge in range(edge_cols):
            start = sender * part_rows * pitch + own_cols - edge_cols + edge
            state_a[pl.ds(start, part_rows, stride=pitch), :] = part[
                part_rows * (8 + edge) : part_rows * (9 + edge)
            ]
        return carry

    def take_main(step, carry):
        sender = nearest(position, step, bit_count)
        main_copy(step, sender).wait_recv()
        part = got[sender, pl.ds(0, main_len), :].astype(jnp.float32)
        for row in range(part_rows):
            start = pl.multiple_of((sender * part_rows + row) * pitch, 8)
            state_a[pl.ds(start, own_cols), :] = part[row * own_cols : (row + 1) * own_cols]
        return carry

    def take_halo(step, carry):
        sender = nearest(position, step, bit_count)
        forwarded(sender).wait_recv()
        mixed = spread(sender, halo[sender], own_cols)
        start = sender * part_rows * pitch + own_cols
        state_a[pl.ds(start + kept_cols, part_rows, stride=pitch), :] = mixed
        state_a[pl.ds(start - 1, part_rows, stride=pitch), :] += jnp.where(lanes < spill_lane, 0.0, mixed)
        return carry

    @pl.when(has_last)
    def _():
        lax.fori_loop(1, group_count, take_first, 0)
        lax.fori_loop(1, group_count, take_rest, 0)

    @pl.when(jnp.logical_not(has_last))
    def _():
        lax.fori_loop(1, group_count, take_main, 0)

    @pl.when(has_next)
    def _():
        lax.fori_loop(0, group_count, take_halo, 0)

    src, dst = state_a, state_b
    for section in range(bit_count):
        level = local_count + section
        local_width = part_rows * 2**section
        log_band = local_width.bit_length()
        merge_level(
            shifts, src, dst, level, rows, pitch, local_width,
            lambda row: (row >> log_band) * 2 ** (level + 1)
            + own_block * (2 * local_width)
            + (row & (2 * local_width - 1)),
            2 * local_width,
        )
        src, dst = dst, src

    scale = 1.0 / math.sqrt(all_channels)
    some = math.gcd(rows, 16)
    for first in range(0, rows, some):
        pieces = [
            jnp.concatenate(
                [
                    (src[pl.ds(row * pitch + lag, own_cols), :] * scale).astype(jnp.bfloat16)
                    for row in range(first, first + some)
                ],
                axis=0,
            )
            for lag in range(tap_count // LANES + 1)
        ]
        result = log_sum(pieces, taps_mat, filter_count)
        for index in range(some):
            row = first + index
            out[pl.ds(row // 8 * 8 * own_cols + row % 8, own_cols, stride=8), :] = result[
                index * own_cols : (index + 1) * own_cols
            ]

    @pl.when(has_last)
    def _():
        def finish_halo(slot, carry):
            forwarded(slot).wait_send()
            return carry

        def finish_parts(step, carry):
            first_copy(step, position).wait_send()
            rest_copy(step, position).wait_send()
            return carry

        lax.fori_loop(0, group_count, finish_halo, 0)
        lax.fori_loop(1, group_count, finish_parts, 0)

    @pl.when(jnp.logical_not(has_last))
    def _():
        def finish_main(step, carry):
            main_copy(step, position).wait_send()
            return carry

        lax.fori_loop(1, group_count, finish_main, 0)


def relay_plan(filterbank, delay_shifts, pulse_filters):
    rows, time_len = filterbank.shape
    sub_count, tm_count = lax.axis_size("sub"), lax.axis_size("tm")
    group_count = lax.axis_size("freq") * sub_count
    level_count = delay_shifts.shape[0]
    tap_count = pulse_filters.shape[1]
    local_count = level_count - (group_count.bit_length() - 1)
    own_cols = time_len // LANES
    reach = 2**level_count - 2**local_count + tap_count - 1
    first_cols = -(-reach // LANES)
    pitch = own_cols + 8
    part_rows = rows // group_count
    fits = (
        part_rows % 8 == 0
        and own_cols % 8 == 0
        and 1 < first_cols < 7
        and first_cols + 7 <= own_cols
        and reach - (first_cols - 1) * LANES <= LANES - 2**local_count
        and tap_count % LANES == 0
        and part_rows * first_cols % 16 == 0
        and 2**level_count // LANES + 2 <= 8
    )
    plan = (rows, time_len, group_count, sub_count, tm_count, own_cols, first_cols, pitch)
    return plan if fits else None


def relayed(plan, filterbank, delay_shifts, pulse_filters):
    rows, time_len, group_count, sub_count, tm_count, own_cols, first_cols, pitch = plan
    filter_count, tap_count = pulse_filters.shape
    part_rows = rows // group_count
    first_len, main_len = part_rows * first_cols, part_rows * own_cols
    spare = 8
    flat = pl.pallas_call(
        functools.partial(relay_kernel, plan),
        out_shape=pltpu.VMEM((rows * own_cols, LANES), jnp.float32),
        in_specs=[pl.BlockSpec(memory_space=pl.ANY)] * 3,
        out_specs=pl.BlockSpec(memory_space=pltpu.VMEM),
        scratch_shapes=[
            pltpu.SMEM(delay_shifts.shape, delay_shifts.dtype),
            pltpu.VMEM(pulse_filters.shape, pulse_filters.dtype),
            pltpu.VMEM(filterbank.shape, filterbank.dtype),
            pltpu.VMEM((rows * own_cols + spare, LANES), jnp.float32),
            pltpu.VMEM((rows * own_cols + spare, LANES), jnp.float32),
            pltpu.VMEM((rows * 8 + spare, LANES), jnp.float32),
            pltpu.VMEM((rows * 8 + spare, LANES), jnp.float32),
            pltpu.VMEM((rows * pitch + spare, LANES), jnp.float32),
            pltpu.VMEM((rows * pitch + spare, LANES), jnp.float32),
            pltpu.VMEM((rows * first_cols + spare, LANES), jnp.float32),
            pltpu.VMEM((group_count * (first_len + 8), LANES), jnp.float32),
            pltpu.VMEM((group_count, main_len + first_len, LANES), WIRE),
            pltpu.VMEM((group_count, main_len + first_len, LANES), WIRE),
            pltpu.VMEM((group_count, first_len, LANES), WIRE),
            pltpu.VMEM((filter_count * LANES, tap_count + LANES), jnp.bfloat16),
        ]
        + [pltpu.SemaphoreType.DMA((group_count,)) for unused in range(6)]
        + [pltpu.SemaphoreType.DMA((3,))],
        compiler_params=pltpu.CompilerParams(collective_id=0, has_side_effects=True),
        name="dedisperse",
    )(delay_shifts, pulse_filters, filterbank)
    tiled = flat.reshape(rows // 8, own_cols, 8, LANES)
    return tiled.transpose(0, 2, 1, 3).reshape(rows, time_len)


def log_sum(pieces, taps_mat, filter_count):
    response = lax.dot_general(
        jnp.concatenate(pieces, axis=1),
        taps_mat[...],
        (((1,), (1,)), ((), ())),
        preferred_element_type=jnp.float32,
    )
    energies = []
    for width in range(filter_count):
        part = response[:, width * LANES : (width + 1) * LANES]
        energies.append(0.5 * part * part)
    top = functools.reduce(jnp.maximum, energies)
    total = functools.reduce(jnp.add, [jnp.exp(energy - top) for energy in energies])
    return jnp.log(total) + top


def local(filterbank, delay_shifts, pulse_filters):
    plan = relay_plan(filterbank, delay_shifts, pulse_filters)
    if plan is not None:
        return relayed(plan, filterbank, delay_shifts, pulse_filters)
    rows, time_len = filterbank.shape
    sub_count, tm_count = lax.axis_size("sub"), lax.axis_size("tm")
    group_count = lax.axis_size("freq") * sub_count
    level_count = delay_shifts.shape[0]
    filter_count, tap_count = pulse_filters.shape
    margin_len = 2**level_count - 1 + tap_count
    takes = margin_takes(time_len, margin_len, tm_count)
    pitch = round_up(-(-(time_len + margin_len) // LANES), 8)
    own_cols = time_len // LANES
    local_count = level_count - (group_count.bit_length() - 1)
    main_pitch = round_up(own_cols, 8)
    main_keep = own_cols - -(-(2**local_count - 1) // LANES)
    tail_pitch = round_up(-(-(time_len + margin_len) // LANES) - main_keep, 8)
    pitch = max(pitch, round_up(main_keep + tail_pitch, 8))
    part_rows = rows // group_count
    main_part = round_up(part_rows * main_pitch, 16)
    tail_part = round_up(part_rows * tail_pitch, 16)
    spare = round_up(2**level_count // LANES + 2, 8)
    plan = (
        rows, time_len, group_count, sub_count, tm_count, takes, pitch, main_pitch, tail_pitch, main_keep,
    )
    reach = time_len // LANES + tap_count // LANES
    return pl.pallas_call(
        functools.partial(kernel, plan),
        out_shape=pltpu.VMEM((rows, time_len), jnp.float32),
        in_specs=[pl.BlockSpec(memory_space=pl.ANY)] * 3,
        out_specs=pl.BlockSpec(memory_space=pltpu.VMEM),
        scratch_shapes=[
            pltpu.SMEM(delay_shifts.shape, delay_shifts.dtype),
            pltpu.VMEM(pulse_filters.shape, pulse_filters.dtype),
            pltpu.VMEM(filterbank.shape, filterbank.dtype),
            pltpu.VMEM((rows * main_pitch + spare, LANES), jnp.float32),
            pltpu.VMEM((rows * main_pitch + spare, LANES), jnp.float32),
            pltpu.VMEM((rows * tail_pitch + spare, LANES), jnp.float32),
            pltpu.VMEM((rows * tail_pitch + spare, LANES), jnp.float32),
            pltpu.VMEM((rows * pitch + spare, LANES), jnp.float32),
            pltpu.VMEM((rows * pitch + spare, LANES), jnp.float32),
            pltpu.VMEM((rows, max(sum(takes), LANES)), jnp.bfloat16),
            pltpu.VMEM((group_count, main_part, LANES), WIRE),
            pltpu.VMEM((group_count, main_part, LANES), WIRE),
            pltpu.VMEM((group_count, tail_part, LANES), WIRE),
            pltpu.VMEM((group_count, tail_part, LANES), WIRE),
            pltpu.VMEM((reach * rows, LANES), jnp.bfloat16),
            pltpu.VMEM((filter_count * LANES, tap_count + LANES), jnp.bfloat16),
            pltpu.SemaphoreType.DMA((max(len(takes), 1),)),
            pltpu.SemaphoreType.DMA((max(len(takes), 1),)),
            pltpu.SemaphoreType.DMA((group_count,)),
            pltpu.SemaphoreType.DMA((group_count,)),
            pltpu.SemaphoreType.DMA((group_count,)),
            pltpu.SemaphoreType.DMA((group_count,)),
            pltpu.SemaphoreType.DMA((3,)),
        ],
        compiler_params=pltpu.CompilerParams(collective_id=0, has_side_effects=True),
        name="dedisperse",
    )(delay_shifts, pulse_filters, filterbank)


def solution(mesh):
    in_specs = (P(("beams", "freq", "sub"), "tm"), P(), P())
    out_specs = P(("beams", "freq", "sub"), "tm")
    return jax.shard_map(local, mesh=mesh, in_specs=in_specs, out_specs=out_specs, check_vma=False)
```

```python
import functools
import math

import jax
import jax.numpy as jnp
from jax import lax
from jax.experimental import pallas as pl
from jax.experimental.pallas import tpu as pltpu
from jax.sharding import PartitionSpec as P

LANES = 128
PAIRS = 32
WIRE = jnp.bfloat16
EARLY = 2


def round_up(value, step):
    return -(-value // step) * step


def margin_takes(time_len, margin_len, tm_count):
    takes = []
    collected = 0
    for unused in range(min(tm_count - 1, -(-margin_len // time_len))):
        take = min(time_len, round_up(margin_len - collected, LANES))
        takes.append(take)
        collected += take
    return takes


def bit_reverse(value, bit_count):
    result = jnp.int32(0)
    for unused in range(bit_count):
        result = result * 2 + value % 2
        value = value // 2
    return result


def merge_level(
    shifts, src, dst, level, rows, pitch, local_width, flat_of, run, closed=False, own_trials=False, base_row=None
):
    lanes = lax.broadcasted_iota(jnp.int32, (pitch, LANES), 1)
    log_width = local_width.bit_length() - 1
    far = 2**level >= LANES
    inside = lax.broadcasted_iota(jnp.int32, (pitch, LANES), 0) < pitch - 1
    pairs = rows // 2
    unroll = min(PAIRS, pairs)
    own_trials = own_trials and unroll % local_width == 0
    base_row = 0 if base_row is None else base_row
    run = min(run, 2 * unroll)

    def body(step, carry):
        first = step * unroll
        base = base_row + first + (first >> log_width) * local_width
        for offset in range(unroll):
            pair = first + offset
            lower = base + offset + (offset >> log_width) * local_width
            upper = lower + local_width
            kept = src[pl.ds(pl.multiple_of(lower * pitch, 8), pitch), :]
            mixed, turns = [], []
            for side in range(2):
                if (2 * offset + side) % run == 0:
                    flat = flat_of(base_row + 2 * pair)
                    table = shifts.at[level, pl.ds(pl.multiple_of(flat, run), run)]
                amount = table[(2 * offset + side) % run]
                start = pl.multiple_of(upper * pitch, 8)
                if far:
                    start = start + (amount >> 7)
                    amount = amount & (LANES - 1)
                here = src[pl.ds(start, pitch), :]
                after = src[pl.ds(start + 1, pitch), :]
                if closed:
                    after = jnp.where(inside, after, 0.0)
                turns.append((LANES - amount) & (LANES - 1))
                still = own_trials and side == 0 and offset % local_width == 0
                mixed.append(here if still else jnp.where(lanes >= amount, here, after))
                if still:
                    turns[-1] = None
            for piece in range(0, pitch, 8):
                moved = [
                    value[piece : piece + 8] if turn is None else pltpu.roll(value[piece : piece + 8], turn, 1)
                    for value, turn in zip(mixed, turns)
                ]
                for side in range(2):
                    out_row = base_row + 2 * pair + side
                    dst[pl.ds(pl.multiple_of(out_row * pitch, 8) + piece, 8), :] = (
                        kept[piece : piece + 8] + moved[side]
                    )
        return carry

    if pairs == unroll:
        body(0, 0)
    else:
        lax.fori_loop(0, pairs // unroll, body, 0)


def kernel(
    plan, shifts_in, filters_in, bank_in, out, shifts, filters, bank, main_a, main_b, tail_a, tail_b, state_a, state_b, margin,
    main_sent, main_got, tail_sent, tail_got, blocks, taps_mat,
    margin_send, margin_recv, main_send, main_recv, tail_send, tail_recv, loaded,
):
    rows, time_len, group_count, sub_count, tm_count, takes, pitch, main_pitch, tail_pitch, main_keep = plan
    level_count, all_channels = shifts.shape
    filter_count, tap_count = filters.shape
    bit_count = group_count.bit_length() - 1
    local_count = level_count - bit_count
    part_rows = rows // group_count
    freq, sub, tm = lax.axis_index("freq"), lax.axis_index("sub"), lax.axis_index("tm")
    position = freq * sub_count + sub
    own_block = bit_reverse(position, bit_count)
    hops = len(takes)

    barrier = pltpu.get_barrier_semaphore()

    def greet(step, carry):
        peer = (position + step) % group_count
        pl.semaphore_signal(
            barrier,
            inc=1,
            device_id={"freq": peer // sub_count, "sub": peer % sub_count},
            device_id_type=pl.DeviceIdType.MESH,
        )
        return carry

    for hop in range(1, hops + 1):
        for way in (-hop, hop):

            @pl.when((tm + way >= 0) & (tm + way < tm_count))
            def _():
                pl.semaphore_signal(
                    barrier, inc=1, device_id={"tm": tm + way}, device_id_type=pl.DeviceIdType.MESH
                )

    lax.fori_loop(1, group_count, greet, 0)

    loads = [
        pltpu.make_async_copy(source, target, loaded.at[index])
        for index, (source, target) in enumerate(
            ((bank_in, bank), (shifts_in, shifts), (filters_in, filters))
        )
    ]
    for load in loads:
        load.start()
    for load in loads:
        load.wait()

    own_cols = time_len // LANES
    for col in range(own_cols):
        main_a[pl.ds(col, rows, stride=main_pitch), :] = bank[:, pl.ds(col * LANES, LANES)].astype(
            jnp.float32
        )
    for col in range(main_keep, own_cols):
        tail_a[pl.ds(col - main_keep, rows, stride=tail_pitch), :] = bank[
            :, pl.ds(col * LANES, LANES)
        ].astype(jnp.float32)

    def local_level(level, ends, ends_pitch):
        src, dst = ends[level % 2], ends[1 - level % 2]
        merge_level(
            shifts, src, dst, level, rows, ends_pitch, 2**level, lambda row: position * rows + row,
            math.gcd(rows, LANES),
        )

    early = min(EARLY, local_count)
    for level in range(early):
        local_level(level, (main_a, main_b), main_pitch)

    neighbours = jnp.minimum(tm, hops) + jnp.minimum(tm_count - 1 - tm, hops)
    pl.semaphore_wait(barrier, group_count - 1 + neighbours)

    def margin_copy(hop):
        offset = sum(takes[: hop - 1])
        return pltpu.make_async_remote_copy(
            src_ref=bank.at[:, pl.ds(0, takes[hop - 1])],
            dst_ref=margin.at[:, pl.ds(offset, takes[hop - 1])],
            send_sem=margin_send.at[hop - 1],
            recv_sem=margin_recv.at[hop - 1],
            device_id={"tm": tm - hop},
            device_id_type=pl.DeviceIdType.MESH,
        )

    for hop in range(1, hops + 1):

        @pl.when(tm - hop >= 0)
        def _():
            margin_copy(hop).start()

    for level in range(early, local_count):
        local_level(level, (main_a, main_b), main_pitch)

    def packed(source, length, target):
        def pack(step, carry):
            block = bit_reverse((position + step) % group_count, bit_count)
            start = pl.multiple_of(block * length, 8)
            target[step, pl.ds(0, length), :] = source[pl.ds(start, length), :].astype(WIRE)
            return carry

        lax.fori_loop(1, group_count, pack, 0)

    def part_copy(step, slot, source, target, send_sems, recv_sems):
        peer = (position + step) % group_count
        return pltpu.make_async_remote_copy(
            src_ref=source.at[step],
            dst_ref=target.at[slot],
            send_sem=send_sems.at[step],
            recv_sem=recv_sems.at[slot],
            device_id={"freq": peer // sub_count, "sub": peer % sub_count},
            device_id_type=pl.DeviceIdType.MESH,
        )

    main_copy = functools.partial(
        part_copy, source=main_sent, target=main_got, send_sems=main_send, recv_sems=main_recv
    )
    tail_copy = functools.partial(
        part_copy, source=tail_sent, target=tail_got, send_sems=tail_send, recv_sems=tail_recv
    )

    def send_all(make):
        def send(step, carry):
            make(step, position).start()
            return carry

        lax.fori_loop(1, group_count, send, 0)

    main_len, tail_len = part_rows * main_pitch, part_rows * tail_pitch
    main_end, tail_end = (main_a, main_b)[local_count % 2], (tail_a, tail_b)[local_count % 2]
    packed(main_end, main_len, main_sent)
    send_all(main_copy)

    for hop in range(1, hops + 1):
        offset = sum(takes[: hop - 1])
        cols = range(offset // LANES, (offset + takes[hop - 1]) // LANES)

        @pl.when(tm + hop < tm_count)
        def _():
            margin_copy(hop).wait_recv()
            for col in cols:
                tail_a[pl.ds(own_cols - main_keep + col, rows, stride=tail_pitch), :] = margin[
                    :, pl.ds(col * LANES, LANES)
                ].astype(jnp.float32)

        @pl.when(tm + hop >= tm_count)
        def _():
            for col in cols:
                tail_a[pl.ds(own_cols - main_keep + col, rows, stride=tail_pitch), :] = jnp.zeros(
                    (rows, LANES), jnp.float32
                )

    for col in range(own_cols - main_keep + sum(takes) // LANES, tail_pitch):
        tail_a[pl.ds(col, rows, stride=tail_pitch), :] = jnp.zeros((rows, LANES), jnp.float32)

    for level in range(local_count):
        local_level(level, (tail_a, tail_b), tail_pitch)
    packed(tail_end, tail_len, tail_sent)
    send_all(tail_copy)

    span = tap_count + LANES
    all_taps = filters[...].astype(jnp.float32)
    for width in range(filter_count):
        row = jnp.concatenate([all_taps[width : width + 1], jnp.zeros((1, LANES), jnp.float32)], axis=1)
        spread = jnp.broadcast_to(row, (LANES, span))
        turned = pltpu.roll(spread, 0, 1, stride=1, stride_axis=0)
        taps_mat[pl.ds(width * LANES, LANES), :] = turned.astype(jnp.bfloat16)

    def place(group, main_part, tail_part):
        for row in range(part_rows):
            start = pl.multiple_of((group * part_rows + row) * pitch, 8)
            if main_part is not None:
                state_a[pl.ds(start, main_pitch), :] = main_part[row * main_pitch : (row + 1) * main_pitch]
            if tail_part is not None:
                state_a[pl.ds(start + main_keep, tail_pitch), :] = tail_part[
                    row * tail_pitch : (row + 1) * tail_pitch
                ]

    place(
        position,
        main_end[pl.ds(pl.multiple_of(own_block * main_len, 8), main_len), :],
        tail_end[pl.ds(pl.multiple_of(own_block * tail_len, 8), tail_len), :],
    )

    def take_main(step, carry):
        sender = (position + group_count - step) % group_count
        main_copy(step, sender).wait_recv()
        place(sender, main_got[sender, pl.ds(0, main_len), :].astype(jnp.float32), None)
        return carry

    def take_tail(step, carry):
        sender = (position + group_count - step) % group_count
        tail_copy(step, sender).wait_recv()
        place(sender, None, tail_got[sender, pl.ds(0, tail_len), :].astype(jnp.float32))
        return carry

    lax.fori_loop(1, group_count, take_main, 0)
    lax.fori_loop(1, group_count, take_tail, 0)
    src, dst = state_a, state_b

    for section in range(bit_count):
        level = local_count + section
        local_width = part_rows * 2**section
        log_band = local_width.bit_length()
        merge_level(
            shifts, src, dst, level, rows, pitch, local_width,
            lambda row: (row >> log_band) * 2 ** (level + 1)
            + own_block * (2 * local_width)
            + (row & (2 * local_width - 1)),
            2 * local_width,
        )
        src, dst = dst, src

    scale = 1.0 / math.sqrt(all_channels)
    reach = own_cols + tap_count // LANES
    for col in range(reach):
        blocks[pl.ds(col * rows, rows), :] = (src[pl.ds(col, rows, stride=pitch), :] * scale).astype(
            jnp.bfloat16
        )

    chunk_cols = 4
    chunk = chunk_cols * rows
    for first in range(0, own_cols, chunk_cols):
        pieces = [
            blocks[pl.ds((first + lag) * rows, chunk), :] for lag in range(tap_count // LANES + 1)
        ]
        response = lax.dot_general(
            jnp.concatenate(pieces, axis=1),
            taps_mat[...],
            (((1,), (1,)), ((), ())),
            preferred_element_type=jnp.float32,
        )
        energies = []
        for width in range(filter_count):
            part = response[:, width * LANES : (width + 1) * LANES]
            energies.append(0.5 * part * part)
        top = functools.reduce(jnp.maximum, energies)
        total = functools.reduce(jnp.add, [jnp.exp(energy - top) for energy in energies])
        result = jnp.log(total) + top
        for col in range(chunk_cols):
            out[:, pl.ds((first + col) * LANES, LANES)] = result[col * rows : (col + 1) * rows]

    for hop in range(1, hops + 1):

        @pl.when(tm - hop >= 0)
        def _():
            margin_copy(hop).wait_send()

    def finish(step, carry):
        main_copy(step, position).wait_send()
        tail_copy(step, position).wait_send()
        return carry

    lax.fori_loop(1, group_count, finish, 0)


def nearest(position, step, bit_count):
    result, unit = jnp.int32(0), 1
    for unused in range(bit_count):
        result = result + (position // unit + step // unit) % 2 * unit
        unit *= 2
    return result


def relay_kernel(
    plan, shifts_in, filters_in, bank_in, out, shifts, filters, bank, main_a, main_b, spill_a, spill_b,
    state_a, state_b, first_stage, halo_stage, sent, got, halo, taps_mat, main_send, main_recv,
    first_send, first_recv, halo_send, halo_recv, loaded,
):
    rows, time_len, group_count, sub_count, tm_count, own_cols, first_cols, pitch = plan
    level_count, all_channels = shifts.shape
    filter_count, tap_count = filters.shape
    bit_count = group_count.bit_length() - 1
    local_count = level_count - bit_count
    part_rows = rows // group_count
    freq, sub, tm = lax.axis_index("freq"), lax.axis_index("sub"), lax.axis_index("tm")
    position = freq * sub_count + sub
    own_block = bit_reverse(position, bit_count)
    has_next, has_last = tm + 1 < tm_count, tm > 0
    first_len, main_len = part_rows * first_cols, part_rows * own_cols
    kept_cols = first_cols - 1
    edge_cols = own_cols - kept_cols - 8
    rest_len = round_up(part_rows * (8 + edge_cols), 16)
    lanes = lax.broadcasted_iota(jnp.int32, (part_rows, LANES), 1)
    spill_lane = LANES - 2**local_count

    loads = [
        pltpu.make_async_copy(source, target, loaded.at[index])
        for index, (source, target) in enumerate(
            ((bank_in, bank), (shifts_in, shifts), (filters_in, filters))
        )
    ]
    for load in loads:
        load.start()

    barrier = pltpu.get_barrier_semaphore()

    def greet(step, carry):
        peer = (position + step) % group_count
        pl.semaphore_signal(
            barrier,
            inc=1,
            device_id={"freq": peer // sub_count, "sub": peer % sub_count},
            device_id_type=pl.DeviceIdType.MESH,
        )
        return carry

    lax.fori_loop(1, group_count, greet, 0)
    for way, present in ((-1, has_last), (1, has_next)):

        @pl.when(present)
        def _():
            pl.semaphore_signal(
                barrier, inc=1, device_id={"tm": tm + way}, device_id_type=pl.DeviceIdType.MESH
            )

    for load in loads:
        load.wait()

    def local_levels(ends, ends_pitch, closed):
        for level in range(local_count):
            merge_level(
                shifts, ends[level % 2], ends[1 - level % 2], level, rows, ends_pitch, 2**level,
                lambda row: position * rows + row, math.gcd(rows, LANES), closed, True,
            )
        return ends[local_count % 2]

    def part_copy(step, slot, send_sems, recv_sems, start, length):
        peer = step - 1 + jnp.where(step - 1 >= position, 1, 0)
        return pltpu.make_async_remote_copy(
            src_ref=sent.at[bit_reverse(peer, bit_count), pl.ds(start, length)],
            dst_ref=got.at[slot, pl.ds(start, length)],
            send_sem=send_sems.at[step],
            recv_sem=recv_sems.at[slot],
            device_id={"freq": peer // sub_count, "sub": peer % sub_count},
            device_id_type=pl.DeviceIdType.MESH,
        )

    main_copy = functools.partial(
        part_copy, send_sems=main_send, recv_sems=main_recv, start=0, length=main_len
    )
    rest_copy = functools.partial(
        part_copy, send_sems=main_send, recv_sems=main_recv, start=0, length=rest_len
    )
    first_copy = functools.partial(
        part_copy, send_sems=first_send, recv_sems=first_recv, start=main_len, length=first_len
    )

    def send_all(make):
        def send(step, carry):
            make(step, position).start()
            return carry

        lax.fori_loop(1, group_count, send, 0)

    def halo_copy(slot, source):
        return pltpu.make_async_remote_copy(
            src_ref=source,
            dst_ref=halo.at[slot],
            send_sem=halo_send.at[slot],
            recv_sem=halo_recv.at[slot],
            device_id={"tm": tm - 1},
            device_id_type=pl.DeviceIdType.MESH,
        )

    def wait_all():
        neighbours = jnp.where(has_last, 1, 0) + jnp.where(has_next, 1, 0)
        pl.semaphore_wait(barrier, group_count - 1 + neighbours)

    @pl.when(has_last)
    def _():
        spill_a[pl.ds(0, rows, stride=8), :] = jnp.zeros((rows, LANES), jnp.float32)
        for col in range(7):
            spill_a[pl.ds(col + 1, rows, stride=8), :] = bank[:, pl.ds(col * LANES, LANES)].astype(
                jnp.float32
            )
        spill_end = local_levels((spill_a, spill_b), 8, False)
        for row in range(rows):
            first_stage[pl.ds(row * first_cols, 8), :] = spill_end[pl.ds(row * 8, 8), :]
        wide = lax.broadcasted_iota(jnp.int32, (rows, LANES), 1)
        first_stage[pl.ds(0, rows, stride=first_cols), :] = jnp.where(
            wide < spill_lane,
            spill_end[pl.ds(first_cols, rows, stride=8), :],
            spill_end[pl.ds(0, rows, stride=8), :],
        )
        for block in range(group_count):
            sent[block, pl.ds(main_len, first_len), :] = first_stage[
                pl.ds(block * first_len, first_len), :
            ].astype(WIRE)
        wait_all()
        send_all(first_copy)
        halo_copy(position, sent.at[own_block, pl.ds(main_len, first_len)]).start()

    for col in range(own_cols):
        main_a[pl.ds(col, rows, stride=own_cols), :] = bank[:, pl.ds(col * LANES, LANES)].astype(
            jnp.float32
        )
    main_end = local_levels((main_a, main_b), own_cols, True)

    @pl.when(jnp.logical_not(has_last))
    def _():
        for block in range(group_count):
            sent[block, pl.ds(0, main_len), :] = main_end[pl.ds(block * main_len, main_len), :].astype(WIRE)
        wait_all()
        send_all(main_copy)

    @pl.when(has_last)
    def _():
        for block in range(group_count):
            first = block * part_rows
            pieces = [
                main_end[pl.ds((first + row) * own_cols + kept_cols, 8), :] for row in range(part_rows)
            ]
            for col in range(own_cols - edge_cols, own_cols):
                pieces.append(main_end[pl.ds(first * own_cols + col, part_rows, stride=own_cols), :])
            for unused in range((rest_len - part_rows * (8 + edge_cols)) // 8):
                pieces.append(jnp.zeros((8, LANES), jnp.float32))
            sent[block, pl.ds(0, rest_len), :] = jnp.concatenate(pieces, axis=0).astype(WIRE)
        send_all(rest_copy)

    span = tap_count + LANES
    all_taps = filters[...].astype(jnp.float32)
    for width in range(filter_count):
        row = jnp.concatenate([all_taps[width : width + 1], jnp.zeros((1, LANES), jnp.float32)], axis=1)
        spread = jnp.broadcast_to(row, (LANES, span))
        turned = pltpu.roll(spread, 0, 1, stride=1, stride_axis=0)
        taps_mat[pl.ds(width * LANES, LANES), :] = turned.astype(jnp.bfloat16)

    for row in range(part_rows):
        start = pl.multiple_of((position * part_rows + row) * pitch, 8)
        state_a[pl.ds(start, own_cols), :] = main_end[
            pl.ds(pl.multiple_of((own_block * part_rows + row) * own_cols, 8), own_cols), :
        ]

    @pl.when(jnp.logical_not(has_next))
    def _():
        for row in range(rows):
            state_a[pl.ds(row * pitch + own_cols, pitch - own_cols), :] = jnp.zeros(
                (pitch - own_cols, LANES), jnp.float32
            )

    def spread(group, part, col):
        base = pl.multiple_of(group * (first_len + 8), 8)
        halo_stage[pl.ds(base, first_len), :] = part.astype(jnp.float32)
        for row in range(part_rows):
            start = (group * part_rows + row) * pitch + col
            state_a[pl.ds(start, 8), :] = halo_stage[pl.ds(base + row * first_cols + 1, 8), :]
        return halo_stage[pl.ds(base, part_rows, stride=first_cols), :]

    def forwarded(sender):
        return halo_copy(sender, got.at[sender, pl.ds(main_len, first_len)])

    def take_first(step, carry):
        sender = nearest(position, step, bit_count)
        first_copy(step, sender).wait_recv()
        forwarded(sender).start()
        spread(sender, got[sender, pl.ds(main_len, first_len), :], 0)
        return carry

    def take_rest(step, carry):
        sender = nearest(position, step, bit_count)
        rest_copy(step, sender).wait_recv()
        part = got[sender, pl.ds(0, rest_len), :].astype(jnp.float32)
        for row in range(part_rows):
            start = (sender * part_rows + row) * pitch + kept_cols
            state_a[pl.ds(start, 8), :] = part[row * 8 : (row + 1) * 8]
        for edge in range(edge_cols):
            start = sender * part_rows * pitch + own_cols - edge_cols + edge
            state_a[pl.ds(start, part_rows, stride=pitch), :] = part[
                part_rows * (8 + edge) : part_rows * (9 + edge)
            ]
        return carry

    def take_main(step, carry):
        sender = nearest(position, step, bit_count)
        main_copy(step, sender).wait_recv()
        part = got[sender, pl.ds(0, main_len), :].astype(jnp.float32)
        for row in range(part_rows):
            start = pl.multiple_of((sender * part_rows + row) * pitch, 8)
            state_a[pl.ds(start, own_cols), :] = part[row * own_cols : (row + 1) * own_cols]
        return carry

    def take_halo(step, carry):
        sender = nearest(position, step, bit_count)
        forwarded(sender).wait_recv()
        mixed = spread(sender, halo[sender], own_cols)
        start = sender * part_rows * pitch + own_cols
        state_a[pl.ds(start + kept_cols, part_rows, stride=pitch), :] = mixed
        state_a[pl.ds(start - 1, part_rows, stride=pitch), :] += jnp.where(lanes < spill_lane, 0.0, mixed)
        return carry

    @pl.when(has_last)
    def _():
        lax.fori_loop(1, group_count, take_first, 0)
        lax.fori_loop(1, group_count, take_rest, 0)

    @pl.when(jnp.logical_not(has_last))
    def _():
        lax.fori_loop(1, group_count, take_main, 0)

    @pl.when(has_next)
    def _():
        lax.fori_loop(0, group_count, take_halo, 0)

    src, dst = state_a, state_b
    for section in range(bit_count):
        level = local_count + section
        local_width = part_rows * 2**section
        log_band = local_width.bit_length()
        merge_level(
            shifts, src, dst, level, rows, pitch, local_width,
            lambda row: (row >> log_band) * 2 ** (level + 1)
            + own_block * (2 * local_width)
            + (row & (2 * local_width - 1)),
            2 * local_width,
        )
        src, dst = dst, src

    scale = 1.0 / math.sqrt(all_channels)
    some = math.gcd(rows, 16)
    for first in range(0, rows, some):
        pieces = [
            jnp.concatenate(
                [
                    (src[pl.ds(row * pitch + lag, own_cols), :] * scale).astype(jnp.bfloat16)
                    for row in range(first, first + some)
                ],
                axis=0,
            )
            for lag in range(tap_count // LANES + 1)
        ]
        result = log_sum(pieces, taps_mat, filter_count)
        for index in range(some):
            row = first + index
            out[pl.ds(row // 8 * 8 * own_cols + row % 8, own_cols, stride=8), :] = result[
                index * own_cols : (index + 1) * own_cols
            ]

    @pl.when(has_last)
    def _():
        def finish_halo(slot, carry):
            forwarded(slot).wait_send()
            return carry

        def finish_parts(step, carry):
            first_copy(step, position).wait_send()
            rest_copy(step, position).wait_send()
            return carry

        lax.fori_loop(0, group_count, finish_halo, 0)
        lax.fori_loop(1, group_count, finish_parts, 0)

    @pl.when(jnp.logical_not(has_last))
    def _():
        def finish_main(step, carry):
            main_copy(step, position).wait_send()
            return carry

        lax.fori_loop(1, group_count, finish_main, 0)


def relay_plan(filterbank, delay_shifts, pulse_filters):
    rows, time_len = filterbank.shape
    sub_count, tm_count = lax.axis_size("sub"), lax.axis_size("tm")
    group_count = lax.axis_size("freq") * sub_count
    level_count = delay_shifts.shape[0]
    tap_count = pulse_filters.shape[1]
    local_count = level_count - (group_count.bit_length() - 1)
    own_cols = time_len // LANES
    reach = 2**level_count - 2**local_count + tap_count - 1
    first_cols = -(-reach // LANES)
    pitch = own_cols + 8
    part_rows = rows // group_count
    fits = (
        part_rows % 8 == 0
        and own_cols % 8 == 0
        and 1 < first_cols < 7
        and first_cols + 7 <= own_cols
        and reach - (first_cols - 1) * LANES <= LANES - 2**local_count
        and tap_count % LANES == 0
        and part_rows * first_cols % 16 == 0
        and 2**level_count // LANES + 2 <= 8
    )
    plan = (rows, time_len, group_count, sub_count, tm_count, own_cols, first_cols, pitch)
    return plan if fits else None


def relayed(plan, filterbank, delay_shifts, pulse_filters):
    rows, time_len, group_count, sub_count, tm_count, own_cols, first_cols, pitch = plan
    filter_count, tap_count = pulse_filters.shape
    part_rows = rows // group_count
    first_len, main_len = part_rows * first_cols, part_rows * own_cols
    spare = 8
    flat = pl.pallas_call(
        functools.partial(relay_kernel, plan),
        out_shape=pltpu.VMEM((rows * own_cols, LANES), jnp.float32),
        in_specs=[pl.BlockSpec(memory_space=pl.ANY)] * 3,
        out_specs=pl.BlockSpec(memory_space=pltpu.VMEM),
        scratch_shapes=[
            pltpu.SMEM(delay_shifts.shape, delay_shifts.dtype),
            pltpu.VMEM(pulse_filters.shape, pulse_filters.dtype),
            pltpu.VMEM(filterbank.shape, filterbank.dtype),
            pltpu.VMEM((rows * own_cols + spare, LANES), jnp.float32),
            pltpu.VMEM((rows * own_cols + spare, LANES), jnp.float32),
            pltpu.VMEM((rows * 8 + spare, LANES), jnp.float32),
            pltpu.VMEM((rows * 8 + spare, LANES), jnp.float32),
            pltpu.VMEM((rows * pitch + spare, LANES), jnp.float32),
            pltpu.VMEM((rows * pitch + spare, LANES), jnp.float32),
            pltpu.VMEM((rows * first_cols + spare, LANES), jnp.float32),
            pltpu.VMEM((group_count * (first_len + 8), LANES), jnp.float32),
            pltpu.VMEM((group_count, main_len + first_len, LANES), WIRE),
            pltpu.VMEM((group_count, main_len + first_len, LANES), WIRE),
            pltpu.VMEM((group_count, first_len, LANES), WIRE),
            pltpu.VMEM((filter_count * LANES, tap_count + LANES), jnp.bfloat16),
        ]
        + [pltpu.SemaphoreType.DMA((group_count,)) for unused in range(6)]
        + [pltpu.SemaphoreType.DMA((3,))],
        compiler_params=pltpu.CompilerParams(collective_id=0, has_side_effects=True),
        name="dedisperse",
    )(delay_shifts, pulse_filters, filterbank)
    tiled = flat.reshape(rows // 8, own_cols, 8, LANES)
    return tiled.transpose(0, 2, 1, 3).reshape(rows, time_len)


def log_sum(pieces, taps_mat, filter_count):
    response = lax.dot_general(
        jnp.concatenate(pieces, axis=1),
        taps_mat[...],
        (((1,), (1,)), ((), ())),
        preferred_element_type=jnp.float32,
    )
    squares = []
    for width in range(filter_count):
        part = response[:, width * LANES : (width + 1) * LANES]
        squares.append(part * part)
    top = functools.reduce(jnp.maximum, squares)
    half = 0.5 / math.log(2.0)
    total = functools.reduce(jnp.add, [jnp.exp2((square - top) * half) for square in squares])
    return jnp.log(total) + 0.5 * top


def local(filterbank, delay_shifts, pulse_filters):
    plan = relay_plan(filterbank, delay_shifts, pulse_filters)
    if plan is not None:
        return relayed(plan, filterbank, delay_shifts, pulse_filters)
    rows, time_len = filterbank.shape
    sub_count, tm_count = lax.axis_size("sub"), lax.axis_size("tm")
    group_count = lax.axis_size("freq") * sub_count
    level_count = delay_shifts.shape[0]
    filter_count, tap_count = pulse_filters.shape
    margin_len = 2**level_count - 1 + tap_count
    takes = margin_takes(time_len, margin_len, tm_count)
    pitch = round_up(-(-(time_len + margin_len) // LANES), 8)
    own_cols = time_len // LANES
    local_count = level_count - (group_count.bit_length() - 1)
    main_pitch = round_up(own_cols, 8)
    main_keep = own_cols - -(-(2**local_count - 1) // LANES)
    tail_pitch = round_up(-(-(time_len + margin_len) // LANES) - main_keep, 8)
    pitch = max(pitch, round_up(main_keep + tail_pitch, 8))
    part_rows = rows // group_count
    main_part = round_up(part_rows * main_pitch, 16)
    tail_part = round_up(part_rows * tail_pitch, 16)
    spare = round_up(2**level_count // LANES + 2, 8)
    plan = (
        rows, time_len, group_count, sub_count, tm_count, takes, pitch, main_pitch, tail_pitch, main_keep,
    )
    reach = time_len // LANES + tap_count // LANES
    return pl.pallas_call(
        functools.partial(kernel, plan),
        out_shape=pltpu.VMEM((rows, time_len), jnp.float32),
        in_specs=[pl.BlockSpec(memory_space=pl.ANY)] * 3,
        out_specs=pl.BlockSpec(memory_space=pltpu.VMEM),
        scratch_shapes=[
            pltpu.SMEM(delay_shifts.shape, delay_shifts.dtype),
            pltpu.VMEM(pulse_filters.shape, pulse_filters.dtype),
            pltpu.VMEM(filterbank.shape, filterbank.dtype),
            pltpu.VMEM((rows * main_pitch + spare, LANES), jnp.float32),
            pltpu.VMEM((rows * main_pitch + spare, LANES), jnp.float32),
            pltpu.VMEM((rows * tail_pitch + spare, LANES), jnp.float32),
            pltpu.VMEM((rows * tail_pitch + spare, LANES), jnp.float32),
            pltpu.VMEM((rows * pitch + spare, LANES), jnp.float32),
            pltpu.VMEM((rows * pitch + spare, LANES), jnp.float32),
            pltpu.VMEM((rows, max(sum(takes), LANES)), jnp.bfloat16),
            pltpu.VMEM((group_count, main_part, LANES), WIRE),
            pltpu.VMEM((group_count, main_part, LANES), WIRE),
            pltpu.VMEM((group_count, tail_part, LANES), WIRE),
            pltpu.VMEM((group_count, tail_part, LANES), WIRE),
            pltpu.VMEM((reach * rows, LANES), jnp.bfloat16),
            pltpu.VMEM((filter_count * LANES, tap_count + LANES), jnp.bfloat16),
            pltpu.SemaphoreType.DMA((max(len(takes), 1),)),
            pltpu.SemaphoreType.DMA((max(len(takes), 1),)),
            pltpu.SemaphoreType.DMA((group_count,)),
            pltpu.SemaphoreType.DMA((group_count,)),
            pltpu.SemaphoreType.DMA((group_count,)),
            pltpu.SemaphoreType.DMA((group_count,)),
            pltpu.SemaphoreType.DMA((3,)),
        ],
        compiler_params=pltpu.CompilerParams(collective_id=0, has_side_effects=True),
        name="dedisperse",
    )(delay_shifts, pulse_filters, filterbank)


def solution(mesh):
    in_specs = (P(("beams", "freq", "sub"), "tm"), P(), P())
    out_specs = P(("beams", "freq", "sub"), "tm")
    return jax.shard_map(local, mesh=mesh, in_specs=in_specs, out_specs=out_specs, check_vma=False)
```

```python
import functools
import math

import jax
import jax.numpy as jnp
from jax import lax
from jax.experimental import pallas as pl
from jax.experimental.pallas import tpu as pltpu
from jax.sharding import PartitionSpec as P

LANES = 128
PAIRS = 32
WIRE = jnp.bfloat16
EARLY = 2


def round_up(value, step):
    return -(-value // step) * step


def margin_takes(time_len, margin_len, tm_count):
    takes = []
    collected = 0
    for unused in range(min(tm_count - 1, -(-margin_len // time_len))):
        take = min(time_len, round_up(margin_len - collected, LANES))
        takes.append(take)
        collected += take
    return takes


def bit_reverse(value, bit_count):
    result = jnp.int32(0)
    for unused in range(bit_count):
        result = result * 2 + value % 2
        value = value // 2
    return result


def merge_level(
    shifts, src, dst, level, rows, pitch, local_width, flat_of, run, closed=False, own_trials=False, base_row=None,
    window=None,
):
    skip, taken = window or (0, pitch)
    lanes = lax.broadcasted_iota(jnp.int32, (taken, LANES), 1)
    log_width = local_width.bit_length() - 1
    far = 2**level >= LANES
    inside = lax.broadcasted_iota(jnp.int32, (pitch, LANES), 0) < pitch - 1
    pairs = rows // 2
    unroll = min(PAIRS, pairs)
    own_trials = own_trials and unroll % local_width == 0
    base_row = 0 if base_row is None else base_row
    run = min(run, 2 * unroll)

    def body(step, carry):
        first = step * unroll
        base = base_row + first + (first >> log_width) * local_width
        for offset in range(unroll):
            pair = first + offset
            lower = base + offset + (offset >> log_width) * local_width
            upper = lower + local_width
            kept = src[pl.ds(pl.multiple_of(lower * pitch, 8) + skip, taken), :]
            mixed, turns = [], []
            for side in range(2):
                if (2 * offset + side) % run == 0:
                    flat = flat_of(base_row + 2 * pair)
                    table = shifts.at[level, pl.ds(pl.multiple_of(flat, run), run)]
                amount = table[(2 * offset + side) % run]
                start = pl.multiple_of(upper * pitch, 8) + skip
                if far:
                    start = start + (amount >> 7)
                    amount = amount & (LANES - 1)
                here = src[pl.ds(start, taken), :]
                after = src[pl.ds(start + 1, taken), :]
                if closed:
                    after = jnp.where(inside, after, 0.0)
                turns.append((LANES - amount) & (LANES - 1))
                still = own_trials and side == 0 and offset % local_width == 0
                mixed.append(here if still else jnp.where(lanes >= amount, here, after))
                if still:
                    turns[-1] = None
            for piece in range(0, taken, 8):
                moved = [
                    value[piece : piece + 8] if turn is None else pltpu.roll(value[piece : piece + 8], turn, 1)
                    for value, turn in zip(mixed, turns)
                ]
                for side in range(2):
                    out_row = base_row + 2 * pair + side
                    dst[pl.ds(pl.multiple_of(out_row * pitch, 8) + skip + piece, 8), :] = (
                        kept[piece : piece + 8] + moved[side]
                    )
        return carry

    if pairs == unroll:
        body(0, 0)
    else:
        lax.fori_loop(0, pairs // unroll, body, 0)


def kernel(
    plan, shifts_in, filters_in, bank_in, out, shifts, filters, bank, main_a, main_b, tail_a, tail_b, state_a, state_b, margin,
    main_sent, main_got, tail_sent, tail_got, blocks, taps_mat,
    margin_send, margin_recv, main_send, main_recv, tail_send, tail_recv, loaded,
):
    rows, time_len, group_count, sub_count, tm_count, takes, pitch, main_pitch, tail_pitch, main_keep = plan
    level_count, all_channels = shifts.shape
    filter_count, tap_count = filters.shape
    bit_count = group_count.bit_length() - 1
    local_count = level_count - bit_count
    part_rows = rows // group_count
    freq, sub, tm = lax.axis_index("freq"), lax.axis_index("sub"), lax.axis_index("tm")
    position = freq * sub_count + sub
    own_block = bit_reverse(position, bit_count)
    hops = len(takes)

    barrier = pltpu.get_barrier_semaphore()

    def greet(step, carry):
        peer = (position + step) % group_count
        pl.semaphore_signal(
            barrier,
            inc=1,
            device_id={"freq": peer // sub_count, "sub": peer % sub_count},
            device_id_type=pl.DeviceIdType.MESH,
        )
        return carry

    for hop in range(1, hops + 1):
        for way in (-hop, hop):

            @pl.when((tm + way >= 0) & (tm + way < tm_count))
            def _():
                pl.semaphore_signal(
                    barrier, inc=1, device_id={"tm": tm + way}, device_id_type=pl.DeviceIdType.MESH
                )

    lax.fori_loop(1, group_count, greet, 0)

    loads = [
        pltpu.make_async_copy(source, target, loaded.at[index])
        for index, (source, target) in enumerate(
            ((bank_in, bank), (shifts_in, shifts), (filters_in, filters))
        )
    ]
    for load in loads:
        load.start()
    for load in loads:
        load.wait()

    own_cols = time_len // LANES
    for col in range(own_cols):
        main_a[pl.ds(col, rows, stride=main_pitch), :] = bank[:, pl.ds(col * LANES, LANES)].astype(
            jnp.float32
        )
    for col in range(main_keep, own_cols):
        tail_a[pl.ds(col - main_keep, rows, stride=tail_pitch), :] = bank[
            :, pl.ds(col * LANES, LANES)
        ].astype(jnp.float32)

    def local_level(level, ends, ends_pitch):
        src, dst = ends[level % 2], ends[1 - level % 2]
        merge_level(
            shifts, src, dst, level, rows, ends_pitch, 2**level, lambda row: position * rows + row,
            math.gcd(rows, LANES),
        )

    early = min(EARLY, local_count)
    for level in range(early):
        local_level(level, (main_a, main_b), main_pitch)

    neighbours = jnp.minimum(tm, hops) + jnp.minimum(tm_count - 1 - tm, hops)
    pl.semaphore_wait(barrier, group_count - 1 + neighbours)

    def margin_copy(hop):
        offset = sum(takes[: hop - 1])
        return pltpu.make_async_remote_copy(
            src_ref=bank.at[:, pl.ds(0, takes[hop - 1])],
            dst_ref=margin.at[:, pl.ds(offset, takes[hop - 1])],
            send_sem=margin_send.at[hop - 1],
            recv_sem=margin_recv.at[hop - 1],
            device_id={"tm": tm - hop},
            device_id_type=pl.DeviceIdType.MESH,
        )

    for hop in range(1, hops + 1):

        @pl.when(tm - hop >= 0)
        def _():
            margin_copy(hop).start()

    for level in range(early, local_count):
        local_level(level, (main_a, main_b), main_pitch)

    def packed(source, length, target):
        def pack(step, carry):
            block = bit_reverse((position + step) % group_count, bit_count)
            start = pl.multiple_of(block * length, 8)
            target[step, pl.ds(0, length), :] = source[pl.ds(start, length), :].astype(WIRE)
            return carry

        lax.fori_loop(1, group_count, pack, 0)

    def part_copy(step, slot, source, target, send_sems, recv_sems):
        peer = (position + step) % group_count
        return pltpu.make_async_remote_copy(
            src_ref=source.at[step],
            dst_ref=target.at[slot],
            send_sem=send_sems.at[step],
            recv_sem=recv_sems.at[slot],
            device_id={"freq": peer // sub_count, "sub": peer % sub_count},
            device_id_type=pl.DeviceIdType.MESH,
        )

    main_copy = functools.partial(
        part_copy, source=main_sent, target=main_got, send_sems=main_send, recv_sems=main_recv
    )
    tail_copy = functools.partial(
        part_copy, source=tail_sent, target=tail_got, send_sems=tail_send, recv_sems=tail_recv
    )

    def send_all(make):
        def send(step, carry):
            make(step, position).start()
            return carry

        lax.fori_loop(1, group_count, send, 0)

    main_len, tail_len = part_rows * main_pitch, part_rows * tail_pitch
    main_end, tail_end = (main_a, main_b)[local_count % 2], (tail_a, tail_b)[local_count % 2]
    packed(main_end, main_len, main_sent)
    send_all(main_copy)

    for hop in range(1, hops + 1):
        offset = sum(takes[: hop - 1])
        cols = range(offset // LANES, (offset + takes[hop - 1]) // LANES)

        @pl.when(tm + hop < tm_count)
        def _():
            margin_copy(hop).wait_recv()
            for col in cols:
                tail_a[pl.ds(own_cols - main_keep + col, rows, stride=tail_pitch), :] = margin[
                    :, pl.ds(col * LANES, LANES)
                ].astype(jnp.float32)

        @pl.when(tm + hop >= tm_count)
        def _():
            for col in cols:
                tail_a[pl.ds(own_cols - main_keep + col, rows, stride=tail_pitch), :] = jnp.zeros(
                    (rows, LANES), jnp.float32
                )

    for col in range(own_cols - main_keep + sum(takes) // LANES, tail_pitch):
        tail_a[pl.ds(col, rows, stride=tail_pitch), :] = jnp.zeros((rows, LANES), jnp.float32)

    for level in range(local_count):
        local_level(level, (tail_a, tail_b), tail_pitch)
    packed(tail_end, tail_len, tail_sent)
    send_all(tail_copy)

    span = tap_count + LANES
    all_taps = filters[...].astype(jnp.float32)
    for width in range(filter_count):
        row = jnp.concatenate([all_taps[width : width + 1], jnp.zeros((1, LANES), jnp.float32)], axis=1)
        spread = jnp.broadcast_to(row, (LANES, span))
        turned = pltpu.roll(spread, 0, 1, stride=1, stride_axis=0)
        taps_mat[pl.ds(width * LANES, LANES), :] = turned.astype(jnp.bfloat16)

    def place(group, main_part, tail_part):
        for row in range(part_rows):
            start = pl.multiple_of((group * part_rows + row) * pitch, 8)
            if main_part is not None:
                state_a[pl.ds(start, main_pitch), :] = main_part[row * main_pitch : (row + 1) * main_pitch]
            if tail_part is not None:
                state_a[pl.ds(start + main_keep, tail_pitch), :] = tail_part[
                    row * tail_pitch : (row + 1) * tail_pitch
                ]

    place(
        position,
        main_end[pl.ds(pl.multiple_of(own_block * main_len, 8), main_len), :],
        tail_end[pl.ds(pl.multiple_of(own_block * tail_len, 8), tail_len), :],
    )

    def take_main(step, carry):
        sender = (position + group_count - step) % group_count
        main_copy(step, sender).wait_recv()
        place(sender, main_got[sender, pl.ds(0, main_len), :].astype(jnp.float32), None)
        return carry

    def take_tail(step, carry):
        sender = (position + group_count - step) % group_count
        tail_copy(step, sender).wait_recv()
        place(sender, None, tail_got[sender, pl.ds(0, tail_len), :].astype(jnp.float32))
        return carry

    lax.fori_loop(1, group_count, take_main, 0)
    lax.fori_loop(1, group_count, take_tail, 0)
    src, dst = state_a, state_b

    for section in range(bit_count):
        level = local_count + section
        local_width = part_rows * 2**section
        log_band = local_width.bit_length()
        merge_level(
            shifts, src, dst, level, rows, pitch, local_width,
            lambda row: (row >> log_band) * 2 ** (level + 1)
            + own_block * (2 * local_width)
            + (row & (2 * local_width - 1)),
            2 * local_width,
        )
        src, dst = dst, src

    scale = 1.0 / math.sqrt(all_channels)
    reach = own_cols + tap_count // LANES
    for col in range(reach):
        blocks[pl.ds(col * rows, rows), :] = (src[pl.ds(col, rows, stride=pitch), :] * scale).astype(
            jnp.bfloat16
        )

    chunk_cols = 4
    chunk = chunk_cols * rows
    for first in range(0, own_cols, chunk_cols):
        pieces = [
            blocks[pl.ds((first + lag) * rows, chunk), :] for lag in range(tap_count // LANES + 1)
        ]
        response = lax.dot_general(
            jnp.concatenate(pieces, axis=1),
            taps_mat[...],
            (((1,), (1,)), ((), ())),
            preferred_element_type=jnp.float32,
        )
        energies = []
        for width in range(filter_count):
            part = response[:, width * LANES : (width + 1) * LANES]
            energies.append(0.5 * part * part)
        top = functools.reduce(jnp.maximum, energies)
        total = functools.reduce(jnp.add, [jnp.exp(energy - top) for energy in energies])
        result = jnp.log(total) + top
        for col in range(chunk_cols):
            out[:, pl.ds((first + col) * LANES, LANES)] = result[col * rows : (col + 1) * rows]

    for hop in range(1, hops + 1):

        @pl.when(tm - hop >= 0)
        def _():
            margin_copy(hop).wait_send()

    def finish(step, carry):
        main_copy(step, position).wait_send()
        tail_copy(step, position).wait_send()
        return carry

    lax.fori_loop(1, group_count, finish, 0)


def nearest(position, step, bit_count):
    result, unit = jnp.int32(0), 1
    for unused in range(bit_count):
        result = result + (position // unit + step // unit) % 2 * unit
        unit *= 2
    return result


def relay_kernel(
    plan, shifts_in, filters_in, bank_in, out, shifts, near_shifts, filters, bank, main_a, main_b, spill_a, spill_b,
    state_a, state_b, early_a, early_b, first_stage, halo_stage, sent, got, halo, taps_mat, main_send, main_recv,
    first_send, first_recv, halo_send, halo_recv, loaded,
):
    rows, time_len, group_count, sub_count, tm_count, own_cols, first_cols, pitch = plan
    level_count, all_channels = shifts.shape
    filter_count, tap_count = filters.shape
    bit_count = group_count.bit_length() - 1
    local_count = level_count - bit_count
    part_rows = rows // group_count
    freq, sub, tm = lax.axis_index("freq"), lax.axis_index("sub"), lax.axis_index("tm")
    position = freq * sub_count + sub
    own_block = bit_reverse(position, bit_count)
    has_next, has_last = tm + 1 < tm_count, tm > 0
    first_len, main_len = part_rows * first_cols, part_rows * own_cols
    kept_cols = first_cols - 1
    edge_cols = own_cols - kept_cols - 8
    rest_len = round_up(part_rows * (8 + edge_cols), 16)
    lanes = lax.broadcasted_iota(jnp.int32, (part_rows, LANES), 1)
    spill_lane = LANES - 2**local_count

    first_span, rest_span = pl.ds(0, 8 * LANES), pl.ds(8 * LANES, time_len - 8 * LANES)
    near_start = pl.multiple_of(position * rows // LANES * LANES, LANES)
    load_near, load_first, load_rest, load_filters, load_shifts = [
        pltpu.make_async_copy(source, target, loaded.at[index])
        for index, (source, target) in enumerate(
            (
                (shifts_in.at[:, pl.ds(near_start, LANES)], near_shifts),
                (bank_in.at[:, first_span], bank.at[:, first_span]),
                (bank_in.at[:, rest_span], bank.at[:, rest_span]),
                (filters_in, filters),
                (shifts_in, shifts),
            )
        )
    ]
    for load in (load_near, load_first, load_rest, load_filters, load_shifts):
        load.start()

    barrier = pltpu.get_barrier_semaphore()

    def greet(step, carry):
        peer = (position + step) % group_count
        pl.semaphore_signal(
            barrier,
            inc=1,
            device_id={"freq": peer // sub_count, "sub": peer % sub_count},
            device_id_type=pl.DeviceIdType.MESH,
        )
        return carry

    lax.fori_loop(1, group_count, greet, 0)
    for way, present in ((-1, has_last), (1, has_next)):

        @pl.when(present)
        def _():
            pl.semaphore_signal(
                barrier, inc=1, device_id={"tm": tm + way}, device_id_type=pl.DeviceIdType.MESH
            )

    load_near.wait()
    load_first.wait()

    def local_levels(ends, ends_pitch, closed):
        for level in range(local_count):
            merge_level(
                near_shifts, ends[level % 2], ends[1 - level % 2], level, rows, ends_pitch, 2**level,
                lambda row: position * rows % LANES + row, math.gcd(rows, LANES), closed, True,
            )
        return ends[local_count % 2]

    def part_copy(step, slot, send_sems, recv_sems, start, length):
        peer = step - 1 + jnp.where(step - 1 >= position, 1, 0)
        return pltpu.make_async_remote_copy(
            src_ref=sent.at[bit_reverse(peer, bit_count), pl.ds(start, length)],
            dst_ref=got.at[slot, pl.ds(start, length)],
            send_sem=send_sems.at[step],
            recv_sem=recv_sems.at[slot],
            device_id={"freq": peer // sub_count, "sub": peer % sub_count},
            device_id_type=pl.DeviceIdType.MESH,
        )

    main_copy = functools.partial(
        part_copy, send_sems=main_send, recv_sems=main_recv, start=0, length=main_len
    )
    rest_copy = functools.partial(
        part_copy, send_sems=main_send, recv_sems=main_recv, start=0, length=rest_len
    )
    first_copy = functools.partial(
        part_copy, send_sems=first_send, recv_sems=first_recv, start=main_len, length=first_len
    )

    def send_all(make):
        def send(step, carry):
            make(step, position).start()
            return carry

        lax.fori_loop(1, group_count, send, 0)

    def halo_copy(slot, source):
        return pltpu.make_async_remote_copy(
            src_ref=source,
            dst_ref=halo.at[slot],
            send_sem=halo_send.at[slot],
            recv_sem=halo_recv.at[slot],
            device_id={"tm": tm - 1},
            device_id_type=pl.DeviceIdType.MESH,
        )

    def wait_all():
        neighbours = jnp.where(has_last, 1, 0) + jnp.where(has_next, 1, 0)
        pl.semaphore_wait(barrier, group_count - 1 + neighbours)

    @pl.when(has_last)
    def _():
        spill_a[pl.ds(0, rows, stride=8), :] = jnp.zeros((rows, LANES), jnp.float32)
        for col in range(7):
            spill_a[pl.ds(col + 1, rows, stride=8), :] = bank[:, pl.ds(col * LANES, LANES)].astype(
                jnp.float32
            )
        spill_end = local_levels((spill_a, spill_b), 8, False)
        for row in range(rows):
            first_stage[pl.ds(row * first_cols, 8), :] = spill_end[pl.ds(row * 8, 8), :]
        wide = lax.broadcasted_iota(jnp.int32, (rows, LANES), 1)
        first_stage[pl.ds(0, rows, stride=first_cols), :] = jnp.where(
            wide < spill_lane,
            spill_end[pl.ds(first_cols, rows, stride=8), :],
            spill_end[pl.ds(0, rows, stride=8), :],
        )
        for block in range(group_count):
            sent[block, pl.ds(main_len, first_len), :] = first_stage[
                pl.ds(block * first_len, first_len), :
            ].astype(WIRE)
        wait_all()
        send_all(first_copy)
        halo_copy(position, sent.at[own_block, pl.ds(main_len, first_len)]).start()

    load_rest.wait()
    for col in range(own_cols):
        main_a[pl.ds(col, rows, stride=own_cols), :] = bank[:, pl.ds(col * LANES, LANES)].astype(
            jnp.float32
        )
    main_end = local_levels((main_a, main_b), own_cols, True)

    @pl.when(jnp.logical_not(has_last))
    def _():
        for block in range(group_count):
            sent[block, pl.ds(0, main_len), :] = main_end[pl.ds(block * main_len, main_len), :].astype(WIRE)
        wait_all()
        send_all(main_copy)

    @pl.when(has_last)
    def _():
        for block in range(group_count):
            first = block * part_rows
            pieces = [
                main_end[pl.ds((first + row) * own_cols + kept_cols, 8), :] for row in range(part_rows)
            ]
            for col in range(own_cols - edge_cols, own_cols):
                pieces.append(main_end[pl.ds(first * own_cols + col, part_rows, stride=own_cols), :])
            for unused in range((rest_len - part_rows * (8 + edge_cols)) // 8):
                pieces.append(jnp.zeros((8, LANES), jnp.float32))
            sent[block, pl.ds(0, rest_len), :] = jnp.concatenate(pieces, axis=0).astype(WIRE)
        send_all(rest_copy)

    load_filters.wait()
    span = tap_count + LANES
    all_taps = filters[...].astype(jnp.float32)
    for width in range(filter_count):
        row = jnp.concatenate([all_taps[width : width + 1], jnp.zeros((1, LANES), jnp.float32)], axis=1)
        spread = jnp.broadcast_to(row, (LANES, span))
        turned = pltpu.roll(spread, 0, 1, stride=1, stride_axis=0)
        taps_mat[pl.ds(width * LANES, LANES), :] = turned.astype(jnp.bfloat16)

    for row in range(part_rows):
        start = pl.multiple_of((position * part_rows + row) * pitch, 8)
        state_a[pl.ds(start, own_cols), :] = main_end[
            pl.ds(pl.multiple_of((own_block * part_rows + row) * own_cols, 8), own_cols), :
        ]

    @pl.when(jnp.logical_not(has_next))
    def _():
        for row in range(rows):
            state_a[pl.ds(row * pitch + own_cols, pitch - own_cols), :] = jnp.zeros(
                (pitch - own_cols, LANES), jnp.float32
            )

    def spread(group, part, col):
        base = pl.multiple_of(group * (first_len + 8), 8)
        halo_stage[pl.ds(base, first_len), :] = part.astype(jnp.float32)
        for row in range(part_rows):
            start = (group * part_rows + row) * pitch + col
            state_a[pl.ds(start, 8), :] = halo_stage[pl.ds(base + row * first_cols + 1, 8), :]
        return halo_stage[pl.ds(base, part_rows, stride=first_cols), :]

    def forwarded(sender):
        return halo_copy(sender, got.at[sender, pl.ds(main_len, first_len)])

    def take_first(step, carry):
        sender = nearest(position, step, bit_count)
        first_copy(step, sender).wait_recv()
        forwarded(sender).start()
        spread(sender, got[sender, pl.ds(main_len, first_len), :], 0)
        return carry

    def take_rest(step, carry):
        sender = nearest(position, step, bit_count)
        rest_copy(step, sender).wait_recv()
        part = got[sender, pl.ds(0, rest_len), :].astype(jnp.float32)
        for row in range(part_rows):
            start = (sender * part_rows + row) * pitch + kept_cols
            state_a[pl.ds(start, 8), :] = part[row * 8 : (row + 1) * 8]
        for edge in range(edge_cols):
            start = sender * part_rows * pitch + own_cols - edge_cols + edge
            state_a[pl.ds(start, part_rows, stride=pitch), :] = part[
                part_rows * (8 + edge) : part_rows * (9 + edge)
            ]
        return carry

    def take_main(step, carry):
        sender = nearest(position, step, bit_count)
        main_copy(step, sender).wait_recv()
        part = got[sender, pl.ds(0, main_len), :].astype(jnp.float32)
        for row in range(part_rows):
            start = pl.multiple_of((sender * part_rows + row) * pitch, 8)
            state_a[pl.ds(start, own_cols), :] = part[row * own_cols : (row + 1) * own_cols]
        return carry

    def take_halo(step, carry):
        sender = nearest(position, step, bit_count)
        forwarded(sender).wait_recv()
        mixed = spread(sender, halo[sender], own_cols)
        start = sender * part_rows * pitch + own_cols
        state_a[pl.ds(start + kept_cols, part_rows, stride=pitch), :] = mixed
        state_a[pl.ds(start - 1, part_rows, stride=pitch), :] += jnp.where(lanes < spill_lane, 0.0, mixed)
        return carry

    @pl.when(has_last)
    def _():
        lax.fori_loop(1, group_count, take_first, 0)
        lax.fori_loop(1, group_count, take_rest, 0)

    @pl.when(jnp.logical_not(has_last))
    def _():
        lax.fori_loop(1, group_count, take_main, 0)

    scale = 1.0 / math.sqrt(all_channels)
    some = math.gcd(rows, 256 // (own_cols - 8))

    def finish_cols(ends, window, first_col, col_count):
        for section in range(bit_count):
            level = local_count + section
            local_width = part_rows * 2**section
            log_band = local_width.bit_length()
            merge_level(
                shifts, ends[section], ends[section + 1], level, rows, pitch, local_width,
                lambda row: (row >> log_band) * 2 ** (level + 1)
                + own_block * (2 * local_width)
                + (row & (2 * local_width - 1)),
                2 * local_width, window=window,
            )
        src = ends[bit_count]
        for first in range(0, rows, some):
            pieces = [
                jnp.concatenate(
                    [
                        (src[pl.ds(row * pitch + first_col + lag, col_count), :] * scale).astype(jnp.bfloat16)
                        for row in range(first, first + some)
                    ],
                    axis=0,
                )
                for lag in range(tap_count // LANES + 1)
            ]
            result = log_sum(pieces, taps_mat, filter_count)
            for index in range(some):
                row = first + index
                out[
                    pl.ds((row // 8 * own_cols + first_col) * 8 + row % 8, col_count, stride=8), :
                ] = result[index * col_count : (index + 1) * col_count]

    load_shifts.wait()
    early = ([early_a, early_b] * bit_count)[:bit_count]
    finish_cols([state_a] + early, (0, own_cols), 0, own_cols - 8)

    @pl.when(has_next)
    def _():
        lax.fori_loop(0, group_count, take_halo, 0)

    late = ([state_a, state_b] * (bit_count + 1))[: bit_count + 1]
    finish_cols(late, (own_cols - 8, 16), own_cols - 8, 8)

    @pl.when(has_last)
    def _():
        def finish_halo(slot, carry):
            forwarded(slot).wait_send()
            return carry

        def finish_parts(step, carry):
            first_copy(step, position).wait_send()
            rest_copy(step, position).wait_send()
            return carry

        lax.fori_loop(0, group_count, finish_halo, 0)
        lax.fori_loop(1, group_count, finish_parts, 0)

    @pl.when(jnp.logical_not(has_last))
    def _():
        def finish_main(step, carry):
            main_copy(step, position).wait_send()
            return carry

        lax.fori_loop(1, group_count, finish_main, 0)


def relay_plan(filterbank, delay_shifts, pulse_filters):
    rows, time_len = filterbank.shape
    sub_count, tm_count = lax.axis_size("sub"), lax.axis_size("tm")
    group_count = lax.axis_size("freq") * sub_count
    level_count = delay_shifts.shape[0]
    tap_count = pulse_filters.shape[1]
    local_count = level_count - (group_count.bit_length() - 1)
    own_cols = time_len // LANES
    reach = 2**level_count - 2**local_count + tap_count - 1
    first_cols = -(-reach // LANES)
    pitch = own_cols + 8
    part_rows = rows // group_count
    fits = (
        part_rows % 8 == 0
        and LANES % rows == 0
        and own_cols > 8
        and own_cols == 16
        and first_cols <= own_cols - 9
        and own_cols % 8 == 0
        and 1 < first_cols < 7
        and first_cols + 7 <= own_cols
        and reach - (first_cols - 1) * LANES <= LANES - 2**local_count
        and tap_count % LANES == 0
        and part_rows * first_cols % 16 == 0
        and 2**level_count // LANES + 2 <= 8
    )
    plan = (rows, time_len, group_count, sub_count, tm_count, own_cols, first_cols, pitch)
    return plan if fits else None


def relayed(plan, filterbank, delay_shifts, pulse_filters):
    rows, time_len, group_count, sub_count, tm_count, own_cols, first_cols, pitch = plan
    filter_count, tap_count = pulse_filters.shape
    part_rows = rows // group_count
    first_len, main_len = part_rows * first_cols, part_rows * own_cols
    spare = 8
    flat = pl.pallas_call(
        functools.partial(relay_kernel, plan),
        out_shape=pltpu.VMEM((rows * own_cols, LANES), jnp.float32),
        in_specs=[pl.BlockSpec(memory_space=pl.ANY)] * 3,
        out_specs=pl.BlockSpec(memory_space=pltpu.VMEM),
        scratch_shapes=[
            pltpu.SMEM(delay_shifts.shape, delay_shifts.dtype),
            pltpu.SMEM((delay_shifts.shape[0], LANES), delay_shifts.dtype),
            pltpu.VMEM(pulse_filters.shape, pulse_filters.dtype),
            pltpu.VMEM(filterbank.shape, filterbank.dtype),
            pltpu.VMEM((rows * own_cols + spare, LANES), jnp.float32),
            pltpu.VMEM((rows * own_cols + spare, LANES), jnp.float32),
            pltpu.VMEM((rows * 8 + spare, LANES), jnp.float32),
            pltpu.VMEM((rows * 8 + spare, LANES), jnp.float32),
            pltpu.VMEM((rows * pitch + spare, LANES), jnp.float32),
            pltpu.VMEM((rows * pitch + spare, LANES), jnp.float32),
            pltpu.VMEM((rows * pitch + spare, LANES), jnp.float32),
            pltpu.VMEM((rows * pitch + spare, LANES), jnp.float32),
            pltpu.VMEM((rows * first_cols + spare, LANES), jnp.float32),
            pltpu.VMEM((group_count * (first_len + 8), LANES), jnp.float32),
            pltpu.VMEM((group_count, main_len + first_len, LANES), WIRE),
            pltpu.VMEM((group_count, main_len + first_len, LANES), WIRE),
            pltpu.VMEM((group_count, first_len, LANES), WIRE),
            pltpu.VMEM((filter_count * LANES, tap_count + LANES), jnp.bfloat16),
        ]
        + [pltpu.SemaphoreType.DMA((group_count,)) for unused in range(6)]
        + [pltpu.SemaphoreType.DMA((5,))],
        compiler_params=pltpu.CompilerParams(collective_id=0, has_side_effects=True),
        name="dedisperse",
    )(delay_shifts, pulse_filters, filterbank)
    tiled = flat.reshape(rows // 8, own_cols, 8, LANES)
    return tiled.transpose(0, 2, 1, 3).reshape(rows, time_len)


def log_sum(pieces, taps_mat, filter_count):
    response = lax.dot_general(
        jnp.concatenate(pieces, axis=1),
        taps_mat[...],
        (((1,), (1,)), ((), ())),
        preferred_element_type=jnp.float32,
    )
    squares = []
    for width in range(filter_count):
        part = response[:, width * LANES : (width + 1) * LANES]
        squares.append(part * part)
    top = functools.reduce(jnp.maximum, squares)
    half = 0.5 / math.log(2.0)
    total = functools.reduce(jnp.add, [jnp.exp2((square - top) * half) for square in squares])
    return jnp.log(total) + 0.5 * top


def local(filterbank, delay_shifts, pulse_filters):
    plan = relay_plan(filterbank, delay_shifts, pulse_filters)
    if plan is not None:
        return relayed(plan, filterbank, delay_shifts, pulse_filters)
    rows, time_len = filterbank.shape
    sub_count, tm_count = lax.axis_size("sub"), lax.axis_size("tm")
    group_count = lax.axis_size("freq") * sub_count
    level_count = delay_shifts.shape[0]
    filter_count, tap_count = pulse_filters.shape
    margin_len = 2**level_count - 1 + tap_count
    takes = margin_takes(time_len, margin_len, tm_count)
    pitch = round_up(-(-(time_len + margin_len) // LANES), 8)
    own_cols = time_len // LANES
    local_count = level_count - (group_count.bit_length() - 1)
    main_pitch = round_up(own_cols, 8)
    main_keep = own_cols - -(-(2**local_count - 1) // LANES)
    tail_pitch = round_up(-(-(time_len + margin_len) // LANES) - main_keep, 8)
    pitch = max(pitch, round_up(main_keep + tail_pitch, 8))
    part_rows = rows // group_count
    main_part = round_up(part_rows * main_pitch, 16)
    tail_part = round_up(part_rows * tail_pitch, 16)
    spare = round_up(2**level_count // LANES + 2, 8)
    plan = (
        rows, time_len, group_count, sub_count, tm_count, takes, pitch, main_pitch, tail_pitch, main_keep,
    )
    reach = time_len // LANES + tap_count // LANES
    return pl.pallas_call(
        functools.partial(kernel, plan),
        out_shape=pltpu.VMEM((rows, time_len), jnp.float32),
        in_specs=[pl.BlockSpec(memory_space=pl.ANY)] * 3,
        out_specs=pl.BlockSpec(memory_space=pltpu.VMEM),
        scratch_shapes=[
            pltpu.SMEM(delay_shifts.shape, delay_shifts.dtype),
            pltpu.VMEM(pulse_filters.shape, pulse_filters.dtype),
            pltpu.VMEM(filterbank.shape, filterbank.dtype),
            pltpu.VMEM((rows * main_pitch + spare, LANES), jnp.float32),
            pltpu.VMEM((rows * main_pitch + spare, LANES), jnp.float32),
            pltpu.VMEM((rows * tail_pitch + spare, LANES), jnp.float32),
            pltpu.VMEM((rows * tail_pitch + spare, LANES), jnp.float32),
            pltpu.VMEM((rows * pitch + spare, LANES), jnp.float32),
            pltpu.VMEM((rows * pitch + spare, LANES), jnp.float32),
            pltpu.VMEM((rows, max(sum(takes), LANES)), jnp.bfloat16),
            pltpu.VMEM((group_count, main_part, LANES), WIRE),
            pltpu.VMEM((group_count, main_part, LANES), WIRE),
            pltpu.VMEM((group_count, tail_part, LANES), WIRE),
            pltpu.VMEM((group_count, tail_part, LANES), WIRE),
            pltpu.VMEM((reach * rows, LANES), jnp.bfloat16),
            pltpu.VMEM((filter_count * LANES, tap_count + LANES), jnp.bfloat16),
            pltpu.SemaphoreType.DMA((max(len(takes), 1),)),
            pltpu.SemaphoreType.DMA((max(len(takes), 1),)),
            pltpu.SemaphoreType.DMA((group_count,)),
            pltpu.SemaphoreType.DMA((group_count,)),
            pltpu.SemaphoreType.DMA((group_count,)),
            pltpu.SemaphoreType.DMA((group_count,)),
            pltpu.SemaphoreType.DMA((3,)),
        ],
        compiler_params=pltpu.CompilerParams(collective_id=0, has_side_effects=True),
        name="dedisperse",
    )(delay_shifts, pulse_filters, filterbank)


def solution(mesh):
    in_specs = (P(("beams", "freq", "sub"), "tm"), P(), P())
    out_specs = P(("beams", "freq", "sub"), "tm")
    return jax.shard_map(local, mesh=mesh, in_specs=in_specs, out_specs=out_specs, check_vma=False)
```
